128 devices in a mesh: px: 16 (over x, z), py: 8 (over y, core).
Axes of the slice: x: 4, y: 4, z: 4, core: 2. Of those that a mesh axis runs over, the one named last changes fastest.
Arguments:
- coords: float32 [3, 262144], P(None, ('px', 'py')), may hold values from -6 to 6
- displacement: float32 [3, 262144], P(None, ('px', 'py')), may hold values from -3 to 3
- velocity: float32 [3, 262144], P(None, ('px', 'py')), may hold values from -6 to 6
- inv_mass: float32 [262144], P(('px', 'py')), may hold values from 0.5 to 2
- ext_force: float32 [3, 262144], P(None, ('px', 'py')), may hold values from -6 to 6
- thickness: float32 [262144], P(('px', 'py')), may hold values from 0.5 to 2
- stiffness: float32 [12, 12], replicated, may hold values from -12 to 12
- elem_nodes: int32 [4, 262144], P(None, ('px', 'py')), may hold values from 0 to 4095
- block_class: int32 [2048], P(('px', 'py')), may hold values from 0 to 1
- halo_lists: int32 [4, 65536], P(None, ('px', 'py')), may hold values from 0 to 2047
- contact_nodes: int32 [262144], P(('px', 'py')), may hold values from 0 to 2047
- contact_bucket: int32 [262144, 1], P(('px', 'py')), may hold values from 0 to 127; in each aligned block of 2048 rows (0 to 2047, 2048 to 4095, ...) at most 32 rows name the same one
- tile_pairs: int32 [2, 2048], P(None, ('px', 'py')), may hold values from 0 to 31
Outputs:
- disp_out: float32 [3, 262144], P(None, ('px', 'py'))
- vel_out: float32 [3, 262144], P(None, ('px', 'py'))
The draws below stay inside these ranges and needn't reach their ends.
Inputs may be any that keep to these rules, and one draw needn't show every extreme that they name: `elem_nodes`: indices into the device's extended list: 2048 own nodes, then four blocks of 512 received nodes. `halo_lists`: row 0 is sent to the neighbour one lower along px, row 1 one higher along px, row 2 one lower along py, row 3 one higher along py; entries are own node indices. `block_class`: class of each block of 128 consecutive elements. `contact_nodes`: own node indices of the device. `contact_bucket`: among the 2048 rows of one device no bucket is named more than 32 times, and in every draw some device names some bucket exactly 32 times. `tile_pairs`: tile numbers within the device's own bucket.
All inputs are finite; a program needn't handle non-finite values.
Results may differ from the reference program's by a relative error of at most 0.0003.
Values sent between devices are 32-bit elements; how exact they have to be, the bound alone decides.
A program may use at most 64 MiB of HBM per device.

```python
import math
import jax
import jax.numpy as jnp
import numpy as np
from jax import lax

ELEM_DEV = 2048
HALO = 512
CN_DEV = 2048
PAIRS = 16
TILE = 128
EBLK = 128
STEPS = 2
SUBS = 2
NODE_DEV = 2048
CAP = 32
TILES = 32
NODES = 262144
ELEMS = 262144
N_PX = 16
N_PY = 8


def place_ends(values, stream_key, smallest, top_value):
    shape = values.shape
    spot = [jax.random.randint(jax.random.fold_in(stream_key, axis), (), 0, shape[axis]) for axis in range(len(shape))]
    values = values.at[tuple(spot)].set(smallest)
    longest = shape.index(max(shape))
    spot[longest] = (spot[longest] + 1) % shape[longest]
    return values.at[tuple(spot)].set(top_value)


def block_scale(rng, shape, pieces, low, high):
    loudness, own = 1.0, jax.random.fold_in(rng, 6)
    for dim, shards_of in pieces:
        steps = jnp.exp(jax.random.uniform(jax.random.fold_in(own, dim), (shards_of,), jnp.float32, low / len(pieces), high / len(pieces)))
        loudness = loudness * jnp.repeat(steps, shape[dim] // shards_of).reshape([-1 if axis == dim else 1 for axis in range(len(shape))])
    return loudness


def deal_out(key, own, number, rows, number_of, top, most, skew):
    ranking = jax.random.permutation(key, number_of)
    crowded, ordinary = shares(number_of, rows * top, most, skew, True), shares(number_of, rows * top, most, skew, False)
    places = jnp.arange(number_of)

    def named(sizes, offset_by):
        used = int((sizes > 0).sum())
        fixed = max(1, used // 4)
        moved = fixed + (places - fixed + offset_by * (used - fixed)) % max(1, number_of - fixed)
        return jnp.zeros((number_of,), jnp.int32).at[ranking[jnp.where(places < fixed, places, moved)]].set(jnp.asarray(sizes, jnp.int32))

    sizes = jnp.where(number % 4 == 0, named(crowded, number // 4), named(ordinary, number - number // 4 - 1))
    mixed = jax.random.permutation(jax.random.fold_in(own, 3), number_of)
    donor, sink = mixed[0:number_of // 2 * 2:2], mixed[1:number_of // 2 * 2:2]
    margin = jnp.minimum(sizes[donor] - 1, most - sizes[sink]) // 2
    margin = jnp.where((donor == ranking[0]) | (sink == ranking[0]) | (sizes[sink] == 0), 0, jnp.maximum(margin, 0))
    moved = jax.random.randint(jax.random.fold_in(own, 4), (number_of // 2,), 0, 1 << 20) % (margin + 1)
    sizes = sizes.at[donor].add(-moved).at[sink].add(moved)
    items = jnp.searchsorted(jnp.cumsum(sizes), jnp.arange(rows * top), side="right").astype(jnp.int32)
    table = items.reshape(top, rows).T
    table = table[jax.random.permutation(jax.random.fold_in(own, 1), rows)]
    offset_by = jax.random.randint(jax.random.fold_in(own, 2), (rows, 1), 0, top)
    return jnp.take_along_axis(table, (jnp.arange(top)[None, :] + offset_by) % top, axis=1)


def shares(amount, total, bound, skew, full):
    portions = [(1 << 20) // math.isqrt(grade ** skew) + 1 for grade in range(1, amount + 1)]
    largest = bound if full else min(bound, max(-(-total // amount), total * portions[0] // sum(portions)))
    least = 1 if total - largest >= amount - 1 else 0
    holding, surplus = [largest] + [least] * (amount - 1), total - largest - least * (amount - 1)
    while surplus > 0:
        candidates = [i for i in range(1, amount) if holding[i] < largest] or [i for i in range(1, amount) if holding[i] < bound]
        pool, left = sum([portions[i] for i in candidates]), surplus
        for i in candidates:
            more = min(bound - holding[i], max(1, left * portions[i] // pool), surplus)
            holding[i] = holding[i] + more
            surplus = surplus - more
    return np.array(holding)


def gaussian(own_key, extent, scale, most, shards=(), kind=jnp.bfloat16):
    drawn = scale * jax.random.normal(own_key, extent, jnp.float32)
    if shards:
        drawn = drawn * block_scale(own_key, extent, shards, -0.22, 0.18)
    return jnp.clip(drawn, -most, most).astype(kind)


def setup_inputs(seed: int = 0) -> dict:
    key_list = jax.random.split(jax.random.key(seed), 14)
    coords = gaussian(key_list[0], (3, NODES), 1.0, 6.0, ((1, 128),), jnp.float32)
    displacement = gaussian(key_list[1], (3, NODES), 0.5, 3.0, ((1, 128),), jnp.float32)
    velocity = gaussian(key_list[2], (3, NODES), 1.0, 6.0, ((1, 128),), jnp.float32)
    inv_mass = jnp.clip(jnp.exp(math.log(2.0) - 1.3862944 * jax.random.uniform(key_list[3], (NODES,), jnp.float32) ** block_scale(key_list[3], (NODES,), ((0, 128),), -0.2, 0.2)), 0.5, 2.0)
    ext_force = gaussian(key_list[4], (3, NODES), 1.0, 6.0, ((1, 128),), jnp.float32)
    thickness = jnp.clip(jnp.exp(math.log(2.0) - 1.3862944 * jax.random.uniform(key_list[5], (ELEMS,), jnp.float32) ** block_scale(key_list[5], (ELEMS,), ((0, 128),), -0.2, 0.2)), 0.5, 2.0)
    stiffness = gaussian(key_list[6], (12, 12), 3.0, 12.0, (), jnp.float32)
    elem_nodes = place_ends(jax.random.randint(key_list[7], (4, ELEMS), 0, NODE_DEV + 4 * HALO), jax.random.fold_in(key_list[7], 1), 0, (NODE_DEV + 4 * HALO) - 1).astype(jnp.int32)
    block_class = place_ends(jax.random.randint(key_list[8], (ELEMS // EBLK,), 0, 2), jax.random.fold_in(key_list[8], 1), 0, 1).astype(jnp.int32)
    halo_lists = place_ends(jax.random.randint(key_list[9], (4, HALO * N_PX * N_PY), 0, NODE_DEV), jax.random.fold_in(key_list[9], 1), 0, NODE_DEV - 1).astype(jnp.int32)
    contact_nodes = place_ends(jax.random.randint(key_list[10], (CN_DEV * N_PX * N_PY,), 0, NODE_DEV), jax.random.fold_in(key_list[10], 1), 0, NODE_DEV - 1).astype(jnp.int32)
    contact_bucket_keys = jax.random.split(jax.random.fold_in(key_list[11], 1), (CN_DEV * N_PX * N_PY) // CN_DEV)
    contact_bucket_turns = jax.random.permutation(jax.random.fold_in(key_list[11], 3), (CN_DEV * N_PX * N_PY) // CN_DEV)
    contact_bucket = jax.vmap(lambda own, number: deal_out(jax.random.fold_in(key_list[11], 2), own, number, CN_DEV, N_PX * N_PY, 1, CAP, 2))(contact_bucket_keys, contact_bucket_turns).reshape((CN_DEV * N_PX * N_PY, 1))
    tile_pairs = place_ends(jax.random.randint(key_list[12], (2, PAIRS * N_PX * N_PY), 0, TILES), jax.random.fold_in(key_list[12], 1), 0, TILES - 1).astype(jnp.int32)
    return dict(coords=coords, displacement=displacement, velocity=velocity, inv_mass=inv_mass, ext_force=ext_force, thickness=thickness, stiffness=stiffness, elem_nodes=elem_nodes, block_class=block_class, halo_lists=halo_lists, contact_nodes=contact_nodes, contact_bucket=contact_bucket, tile_pairs=tile_pairs)


FAR = 1.0e4
DT = 0.05
PENALTY = 0.5
REACH = 4.0


def split_dev(array_in, width):
    lead = array_in.shape[:-1]
    blocks = array_in.reshape(lead + (N_PX * N_PY, width))
    return jnp.moveaxis(blocks, -2, 0)


def join_dev(blocks):
    moved = jnp.moveaxis(blocks, 0, -2)
    return moved.reshape(moved.shape[:-2] + (moved.shape[-2] * moved.shape[-1],))


def grid_shift(blocks, axis_no, offset):
    length = blocks.shape[axis_no]
    zero_part = jnp.zeros_like(lax.slice_in_dim(blocks, 0, 1, axis=axis_no))
    if offset == 1:
        return jnp.concatenate([zero_part, lax.slice_in_dim(blocks, 0, length - 1, axis=axis_no)], axis_no)
    return jnp.concatenate([lax.slice_in_dim(blocks, 1, length, axis=axis_no), zero_part], axis_no)


def halo_extend(values, lists):
    picked = jax.vmap(lambda field_in, rows_in: field_in[:, rows_in])(values, lists)
    grid = picked.reshape(N_PX, N_PY, 3, 4, HALO)
    from_low_x = grid_shift(grid[:, :, :, 1], 0, 1)
    from_high_x = grid_shift(grid[:, :, :, 0], 0, -1)
    from_low_y = grid_shift(grid[:, :, :, 3], 1, 1)
    from_high_y = grid_shift(grid[:, :, :, 2], 1, -1)
    parts = [blk.reshape(N_PX * N_PY, 3, HALO) for blk in (from_low_x, from_high_x, from_low_y, from_high_y)]
    return jnp.concatenate([values] + parts, axis=2)


def halo_return(force_ext, lists):
    owned_count = NODE_DEV
    blocks = [force_ext[:, :, owned_count + number * HALO: owned_count + (number + 1) * HALO].reshape(N_PX, N_PY, 3, HALO) for number in range(4)]
    back_zero = grid_shift(blocks[1], 0, 1)
    back_one = grid_shift(blocks[0], 0, -1)
    back_two = grid_shift(blocks[3], 1, 1)
    back_three = grid_shift(blocks[2], 1, -1)
    returned = jnp.stack([back_zero, back_one, back_two, back_three], axis=3).reshape(N_PX * N_PY, 3, 4 * HALO)

    def add_back(own_part, ret_part, rows_in):
        return own_part + jnp.zeros((3, owned_count), jnp.float32).at[:, rows_in.reshape(-1)].add(ret_part)

    return jax.vmap(add_back)(force_ext[:, :, :owned_count], returned, lists)


def element_forces(ext_values, elem_nodes, thickness, stiffness):
    corners = ext_values[:, elem_nodes]
    local = corners.reshape(12, elem_nodes.shape[1])
    return thickness[None, :] * jnp.dot(stiffness, local, precision=lax.Precision.HIGHEST)


def assemble(forces, elem_nodes, extended):
    return jnp.zeros((3, extended), jnp.float32).at[:, elem_nodes.reshape(-1)].add(forces.reshape(3, -1))


def contact_slots(bucket, devices, capacity):
    onehot = (bucket[:, None] == jnp.arange(devices, dtype=jnp.int32)[None, :]).astype(jnp.int32)
    before = jnp.cumsum(onehot, axis=0) - onehot
    ranks = jnp.sum(before * onehot, axis=1).astype(jnp.int32)
    return (bucket * capacity + ranks).astype(jnp.int32)


def tile_forces(arrived, tile_pairs):
    tiles = arrived.reshape(3, -1, TILE)

    def one_pair(total, pair):
        first = pair[0]
        second = pair[1]
        pos_a = lax.dynamic_index_in_dim(tiles, first, 1, keepdims=False)
        pos_b = lax.dynamic_index_in_dim(tiles, second, 1, keepdims=False)
        gap = pos_a[:, :, None] - pos_b[:, None, :]
        dist = jnp.sum(gap * gap, axis=0)
        weight = PENALTY * jnp.exp(-dist / REACH)
        push = jnp.sum(weight[None, :, :] * gap, axis=2)
        current = lax.dynamic_index_in_dim(total, first, 1, keepdims=False)
        return lax.dynamic_update_index_in_dim(total, current + push, first, 1), None

    start = jnp.zeros(tiles.shape, jnp.float32)
    total, unused = lax.scan(one_pair, start, tile_pairs.T)
    return total.reshape(3, -1)


def relayout(blocks, devices, capacity):
    grid = blocks.reshape(devices, 3, devices, capacity)
    return jnp.transpose(grid, (2, 1, 0, 3)).reshape(devices, 3, devices * capacity)


def reference(coords, displacement, velocity, inv_mass, ext_force, thickness, stiffness, elem_nodes, block_class, halo_lists, contact_nodes, contact_bucket, tile_pairs):
    devices = N_PX * N_PY
    capacity = 2 * CN_DEV // devices
    width = devices * capacity
    extended = NODE_DEV + 4 * HALO
    base = split_dev(coords, NODE_DEV)
    disp = split_dev(displacement, NODE_DEV)
    vel = split_dev(velocity, NODE_DEV)
    inv_m = split_dev(inv_mass, NODE_DEV)
    f_ext = split_dev(ext_force, NODE_DEV)
    thick = split_dev(thickness, ELEM_DEV)
    enodes = split_dev(elem_nodes, ELEM_DEV)
    slow_elems = jnp.repeat(split_dev(block_class, ELEM_DEV // EBLK), EBLK, axis=1) == 1
    lists = split_dev(halo_lists, HALO)
    cnodes = split_dev(contact_nodes, CN_DEV)
    buckets = contact_bucket[:, 0].reshape(devices, CN_DEV)
    pairs = split_dev(tile_pairs, PAIRS)
    slots = jax.vmap(lambda bucket_row: contact_slots(bucket_row, devices, capacity))(buckets)

    def fill_slots(points, node_ids, slot_ids):
        return jnp.full((3, width), FAR, jnp.float32).at[:, slot_ids].set(points[:, node_ids])

    def take_back(force_in, node_ids, slot_ids):
        return jnp.zeros((3, NODE_DEV), jnp.float32).at[:, node_ids].add(force_in[:, slot_ids])

    for step_no in range(STEPS):
        outgoing = jax.vmap(fill_slots)(base + disp, cnodes, slots)
        arrived = relayout(outgoing, devices, capacity)
        pushes = jax.vmap(tile_forces)(arrived, pairs)
        returned = relayout(pushes, devices, capacity)
        contact = jax.vmap(take_back)(returned, cnodes, slots)
        held_forces = None
        for sub_no in range(SUBS):
            ext_disp = halo_extend(disp, lists)
            forces = jax.vmap(lambda ev, en, th: element_forces(ev, en, th, stiffness))(ext_disp, enodes, thick)
            if sub_no == 0:
                held_forces = forces
            else:
                forces = jnp.where(slow_elems[:, None, :], held_forces, forces)
            summed = jax.vmap(lambda fo, en: assemble(fo, en, extended))(forces, enodes)
            internal = halo_return(summed, lists)
            accel = inv_m[:, None, :] * (f_ext - internal + contact)
            vel = vel + DT * accel
            disp = disp + DT * vel
    return join_dev(disp), join_dev(vel)
```

```python
import jax
import jax.numpy as jnp
from jax import lax
from jax.experimental import pallas as pl
from jax.experimental.pallas import tpu as pltpu
from jax.sharding import PartitionSpec as P

MESH = pl.DeviceIdType.MESH
LANES = 128
EBLK = 128
STEPS = 2
SUBS = 2
FAR = 10000.0
DT = 0.05
PENALTY = 0.5
REACH = 4.0

N_PX = 16
N_PY = 8
DEVS = N_PX * N_PY
NROW = 16
EROW = 16
HROW = 4
XROW = NROW + 4 * HROW
CROW = 16
SROW = 32
CAP = 32
PAIRS = 16
IDXROW = 4 * EROW + 4 * HROW

F32 = jnp.float32
BF16 = jnp.bfloat16
I32 = jnp.int32


def iota(shape, dim):
    return lax.broadcasted_iota(I32, shape, dim)


def pick(row, index):
    return jnp.take_along_axis(
        jnp.broadcast_to(row, index.shape), index, axis=1, mode="promise_in_bounds"
    )


def gather(table, height, first, count, high, low, start):
    def some(step, found):
        for inner in range(4):
            row = first + step * 4 + inner
            here = high == row
            found = tuple(
                jnp.where(here, pick(table[pl.ds(c * height + row, 1), :], low), found[c])
                for c in range(3)
            )
        return found

    return lax.fori_loop(0, count // 4, some, start)


def halves(value):
    upper = value.astype(BF16).astype(F32)
    return upper, value - upper


def scatter(values, rows, high, first, onehot, tile, height):
    numbers = iota((height, LANES), 0)

    def two_rows(step, total):
        columns = []
        for inner in range(2):
            row = step * 2 + inner
            here = jnp.broadcast_to(high[pl.ds(first + row, 1), :], (height, LANES)) == numbers
            uppers, lowers = [], []
            for c in range(3):
                upper, lower = halves(values[pl.ds(c * rows + row, 1), :])
                uppers.append(jnp.where(here, upper, 0.0))
                lowers.append(jnp.where(here, lower, 0.0))
            columns.append(jnp.concatenate(uppers + lowers, axis=0).astype(BF16))
        left = jnp.concatenate(columns, axis=1)
        return total + jnp.dot(left, onehot[tile + step], preferred_element_type=F32)

    total = lax.fori_loop(0, rows // 2, two_rows, jnp.zeros((6 * height, LANES), F32))
    return total[: 3 * height] + total[3 * height :]


def build_onehots(columns, rows, onehot, tile):
    lanes = iota((LANES, LANES), 1)

    def one(row, carry):
        spread = jnp.take_along_axis(
            columns, jnp.full((LANES, LANES), row, I32), axis=1, mode="promise_in_bounds"
        )
        half = pl.multiple_of(lax.rem(row, 2) * LANES, LANES)
        onehot[tile + row // 2, pl.ds(half, LANES), :] = jnp.where(
            spread == lanes, 1.0, 0.0
        ).astype(BF16)
        return carry

    lax.fori_loop(0, rows, one, 0)


def transposed(index):
    padded = jnp.concatenate(
        [index.astype(F32), jnp.zeros((LANES - index.shape[0], LANES), F32)], axis=0
    )
    return jnp.transpose(padded).astype(I32)


def body(
    coords,
    displacement,
    velocity,
    ext_force,
    elem_nodes,
    halo_lists,
    inv_mass,
    thickness,
    contact_nodes,
    bucket,
    stiffness,
    block_class,
    tile_pairs,
    disp_out,
    vel_out,
    base,
    disp,
    vel,
    fext,
    slow,
    idx_low,
    idx_high,
    table,
    forces,
    held,
    internal,
    contact,
    returned,
    onehot,
    named,
    ranks,
    inverse,
    slot_low,
    slot_high,
    points,
    pushes,
    stage,
    halo_out,
    halo_in,
    back_out,
    back_in,
    slots_out,
    slots_in,
    halo_sent,
    halo_got,
    back_sent,
    back_got,
    slots_sent,
    slots_got,
):
    i = lax.axis_index("px")
    j = lax.axis_index("py")
    me = i * N_PY + j
    neighbours = [
        (i > 0, (jnp.maximum(i - 1, 0), j)),
        (i < N_PX - 1, (jnp.minimum(i + 1, N_PX - 1), j)),
        (j > 0, (i, jnp.maximum(j - 1, 0))),
        (j < N_PY - 1, (i, jnp.minimum(j + 1, N_PY - 1))),
    ]
    facing = [1, 0, 3, 2]

    halo_in[...] = jnp.zeros_like(halo_in)
    back_in[...] = jnp.zeros_like(back_in)

    barrier = pltpu.get_barrier_semaphore()

    def greet(k, carry):
        other = lax.rem(me + k, DEVS)
        pl.semaphore_signal(
            barrier,
            inc=1,
            device_id=(other // N_PY, lax.rem(other, N_PY)),
            device_id_type=MESH,
        )
        return carry

    lax.fori_loop(1, DEVS, greet, 0)

    def to_rows(source, target, count, rows):
        for c in range(count):
            for r in range(rows):
                target[pl.ds(c * rows + r, 1), :] = source[
                    pl.ds(c, 1), pl.ds(r * LANES, LANES)
                ]

    to_rows(coords, base, 3, NROW)
    to_rows(displacement, disp, 3, NROW)
    to_rows(velocity, vel, 3, NROW)
    to_rows(ext_force, fext, 3, NROW)
    for k in range(4):
        for r in range(EROW):
            entry = elem_nodes[pl.ds(k, 1), pl.ds(r * LANES, LANES)]
            idx_low[pl.ds(k * EROW + r, 1), :] = entry & (LANES - 1)
            idx_high[pl.ds(k * EROW + r, 1), :] = entry >> 7
    for k in range(4):
        for r in range(HROW):
            entry = halo_lists[pl.ds(k, 1), pl.ds(r * LANES, LANES)]
            idx_low[pl.ds(4 * EROW + k * HROW + r, 1), :] = entry & (LANES - 1)
            idx_high[pl.ds(4 * EROW + k * HROW + r, 1), :] = entry >> 7
    for r in range(EROW):
        slow[pl.ds(r, 1), :] = jnp.full((1, LANES), block_class[r], I32)

    devs = iota((LANES, LANES), 0)
    lanes = iota((LANES, LANES), 1)
    earlier = jnp.concatenate(
        [jnp.where(devs < lanes, 1.0, 0.0), jnp.ones((LANES, LANES), F32)], axis=1
    ).astype(BF16)

    def rank_row(row, before):
        here = jnp.broadcast_to(bucket[pl.ds(row, 1), :], (LANES, LANES)) == devs
        spread = jnp.where(here, 1.0, 0.0).astype(BF16)
        named[row] = spread
        counts = jnp.dot(spread, earlier, preferred_element_type=F32)
        rank = jnp.sum(
            jnp.where(here, counts[:, :LANES] + before, 0.0), axis=0, keepdims=True
        )
        ranks[pl.ds(row, 1), :] = rank.astype(I32)
        return before + counts[:, LANES:]

    lax.fori_loop(0, CROW, rank_row, jnp.zeros((LANES, LANES), F32))

    joined = transposed(ranks[...] + CAP * contact_nodes[...])
    slot_lane = lanes & (CAP - 1)

    def invert_row(row, total):
        spread = jnp.take_along_axis(
            joined, jnp.full((LANES, LANES), row, I32), axis=1, mode="promise_in_bounds"
        )
        here = (spread & (CAP - 1)) == slot_lane
        low = ((spread >> 5) & (LANES - 1)).astype(F32)
        high = ((spread >> 12) + 1).astype(F32)
        right = jnp.concatenate(
            [jnp.where(here, low, 0.0), jnp.where(here, high, 0.0)], axis=1
        ).astype(BF16)
        return total + jnp.dot(named[row], right, preferred_element_type=F32)

    nodes = lax.fori_loop(0, CROW, invert_row, jnp.zeros((LANES, 2 * LANES), F32))
    inverse[pl.ds(0, DEVS), :] = nodes[:, :LANES]
    inverse[pl.ds(DEVS, DEVS), :] = nodes[:, LANES:]
    block = iota((SROW, LANES), 1) >> 5
    low = jnp.zeros((SROW, LANES), F32)
    high = jnp.zeros((SROW, LANES), F32)
    for q in range(4):
        low = jnp.where(block == q, inverse[pl.ds(q, SROW, stride=4), :], low)
        high = jnp.where(block == q, inverse[pl.ds(DEVS + q, SROW, stride=4), :], high)
    slot_low[...] = low.astype(I32)
    slot_high[...] = high.astype(I32) - 1

    def exchange_start(number, source, target, sent, got):
        for n, (exists, device) in enumerate(neighbours):

            @pl.when(exists)
            def _():
                pltpu.make_async_remote_copy(
                    src_ref=source.at[number, n],
                    dst_ref=target.at[number, facing[n]],
                    send_sem=sent.at[number, n],
                    recv_sem=got.at[number, facing[n]],
                    device_id=device,
                    device_id_type=MESH,
                ).start()

    def exchange_wait(number, buffer, sem):
        for n, (exists, _unused) in enumerate(neighbours):

            @pl.when(exists)
            def _():
                pltpu.make_async_copy(
                    buffer.at[number, n], buffer.at[number, n], sem.at[number, n]
                ).wait()

    def slots_start(number):
        def send(k, carry):
            other = lax.rem(me + k, DEVS)
            pltpu.make_async_remote_copy(
                src_ref=slots_out.at[number, other],
                dst_ref=slots_in.at[number, me],
                send_sem=slots_sent.at[number],
                recv_sem=slots_got.at[number],
                device_id=(other // N_PY, lax.rem(other, N_PY)),
                device_id_type=MESH,
            ).start()
            return carry

        lax.fori_loop(1, DEVS, send, 0)
        slots_in[number, me] = slots_out[number, me]

    def slots_wait(number, buffer, sem):
        part = buffer.at[number, pl.ds(0, DEVS - 1)]
        pltpu.make_async_copy(part, part, sem.at[number]).wait()

    def to_messages(parts, number):
        for q in range(4):
            mixed = jnp.zeros((SROW, LANES), F32)
            for c in range(3):
                shift = (CAP * (c - q)) % LANES
                turned = pltpu.roll(parts[c], shift, 1) if shift else parts[c]
                mixed = jnp.where(block == c, turned, mixed)
            stage[pl.ds(q * SROW, SROW), :] = mixed
        for a in range(SROW):
            for q in range(4):
                slots_out[number, 4 * a + q] = stage[pl.ds(q * SROW + a, 1), :]

    def from_messages(number):
        for a in range(SROW):
            for q in range(4):
                stage[pl.ds(q * SROW + a, 1), :] = slots_in[number, 4 * a + q]
        parts = []
        for c in range(3):
            mixed = jnp.zeros((SROW, LANES), F32)
            for q in range(4):
                shift = (CAP * (q - c)) % LANES
                rows = stage[pl.ds(q * SROW, SROW), :]
                turned = pltpu.roll(rows, shift, 1) if shift else rows
                mixed = jnp.where(block == q, turned, mixed)
            parts.append(mixed)
        return parts

    def send_points(number):
        table[pl.ds(0, 3 * NROW), :] = base[...] + disp[...]
        far = jnp.full((SROW, LANES), FAR, F32)
        found = gather(table, NROW, 0, NROW, slot_high[...], slot_low[...], (far, far, far))
        to_messages(found, number)

    def push_tiles(number):
        for c, part in enumerate(from_messages(number)):
            points[pl.ds(c * SROW, SROW), :] = part
        numbers = iota((SROW, LANES), 0)

        def one_pair(p, totals):
            first = tile_pairs[0, p]
            second = tile_pairs[1, p]
            mine = [
                jnp.broadcast_to(points[pl.ds(c * SROW + first, 1), :], (8, LANES))
                for c in range(3)
            ]
            others = [
                jnp.broadcast_to(points[pl.ds(c * SROW + second, 1), :], (8, LANES))
                for c in range(3)
            ]
            sums = [jnp.zeros((8, LANES), F32) for c in range(3)]
            for turn in range(LANES // 8):
                gap = [
                    mine[c] - pltpu.roll(others[c], turn * 8, 1, stride=1, stride_axis=0)
                    for c in range(3)
                ]
                dist = gap[0] * gap[0] + gap[1] * gap[1] + gap[2] * gap[2]
                weight = PENALTY * jnp.exp(dist * (-1.0 / REACH))
                sums = [sums[c] + weight * gap[c] for c in range(3)]
            return tuple(
                totals[c]
                + jnp.where(numbers == first, jnp.sum(sums[c], axis=0, keepdims=True), 0.0)
                for c in range(3)
            )

        zero = jnp.zeros((SROW, LANES), F32)
        return lax.fori_loop(0, PAIRS, one_pair, (zero, zero, zero))

    def send_edges(number):
        for c in range(3):
            table[pl.ds(c * XROW, NROW), :] = disp[pl.ds(c * NROW, NROW), :]
        zero = jnp.zeros((4 * HROW, LANES), F32)
        listed = pl.ds(4 * EROW, 4 * HROW)
        found = gather(
            table, XROW, 0, NROW, idx_high[listed, :], idx_low[listed, :], (zero, zero, zero)
        )
        for n in range(4):
            for c in range(3):
                halo_out[number, n, pl.ds(c * HROW, HROW), :] = found[c][
                    n * HROW : (n + 1) * HROW
                ]
        exchange_start(number, halo_out, halo_in, halo_sent, halo_got)

    def element_stage(number, sub_no):
        corners = pl.ds(0, 4 * EROW)
        zero = jnp.zeros((4 * EROW, LANES), F32)
        found = gather(
            table, XROW, 0, NROW, idx_high[corners, :], idx_low[corners, :], (zero, zero, zero)
        )
        exchange_wait(number, halo_in, halo_got)
        for n in range(4):
            for c in range(3):
                table[pl.ds(c * XROW + NROW + n * HROW, HROW), :] = halo_in[
                    number, n, pl.ds(c * HROW, HROW), :
                ]
        found = gather(
            table, XROW, NROW, 4 * HROW, idx_high[corners, :], idx_low[corners, :], found
        )
        local = [
            found[c][k * EROW : (k + 1) * EROW] for c in range(3) for k in range(4)
        ]
        thick = thickness[...]
        for out in range(12):
            total = stiffness[out, 0] * local[0]
            for of in range(1, 12):
                total = total + stiffness[out, of] * local[of]
            total = thick * total
            place = pl.ds(out * EROW, EROW)
            if sub_no == 0:
                held[place, :] = total
            else:
                total = jnp.where(slow[...] == 1, held[place, :], total)
            forces[place, :] = total
        summed = scatter(forces, 4 * EROW, idx_high, 0, onehot, 0, XROW)
        for c in range(3):
            internal[pl.ds(c * NROW, NROW), :] = summed[c * XROW : c * XROW + NROW]
            for n in range(4):
                first = c * XROW + NROW + n * HROW
                back_out[number, n, pl.ds(c * HROW, HROW), :] = summed[first : first + HROW]
        exchange_start(number, back_out, back_in, back_sent, back_got)

    def return_stage(number):
        exchange_wait(number, back_in, back_got)
        for n in range(4):
            for c in range(3):
                returned[pl.ds(c * 4 * HROW + n * HROW, HROW), :] = back_in[
                    number, n, pl.ds(c * HROW, HROW), :
                ]
        internal[...] = internal[...] + scatter(
            returned, 4 * HROW, idx_high, 4 * EROW, onehot, 2 * EROW, NROW
        )

    def update():
        mass = inv_mass[...]
        for c in range(3):
            place = pl.ds(c * NROW, NROW)
            accel = mass * (fext[place, :] - internal[place, :] + contact[place, :])
            speed = vel[place, :] + DT * accel
            vel[place, :] = speed
            disp[place, :] = disp[place, :] + DT * speed

    def major(step, carry):
        there, back = 2 * step, 2 * step + 1
        send_points(there)

        @pl.when(step == 0)
        def _():
            pl.semaphore_wait(barrier, DEVS - 1)

        slots_start(there)
        send_edges(there)

        @pl.when(step == 0)
        def _():
            build_onehots(transposed(idx_low[...]), IDXROW, onehot, 0)
            build_onehots(transposed(slot_low[...]), SROW, onehot, IDXROW // 2)

        element_stage(there, 0)
        slots_wait(there, slots_in, slots_got)
        to_messages(push_tiles(there), back)
        slots_start(back)
        return_stage(there)
        slots_wait(back, slots_in, slots_got)
        for c, part in enumerate(from_messages(back)):
            pushes[pl.ds(c * SROW, SROW), :] = part
        contact[...] = scatter(pushes, SROW, slot_high, 0, onehot, IDXROW // 2, NROW)
        update()
        for sub_no in range(1, SUBS):
            send_edges(back)
            element_stage(back, sub_no)
            return_stage(back)
            update()
        return carry

    lax.fori_loop(0, STEPS, major, 0)

    for c in range(3):
        for r in range(NROW):
            row = pl.ds(c * NROW + r, 1)
            place = pl.ds(r * LANES, LANES)
            disp_out[pl.ds(c, 1), place] = disp[row, :]
            vel_out[pl.ds(c, 1), place] = vel[row, :]

    def drain(number, carry):
        exchange_wait(number, halo_out, halo_sent)
        exchange_wait(number, back_out, back_sent)
        slots_wait(number, slots_out, slots_sent)
        return carry

    lax.fori_loop(0, STEPS * SUBS, drain, 0)


def device_step(
    coords,
    displacement,
    velocity,
    inv_mass,
    ext_force,
    thickness,
    stiffness,
    elem_nodes,
    block_class,
    halo_lists,
    contact_nodes,
    contact_bucket,
    tile_pairs,
):
    times = STEPS * SUBS
    vmem = pl.BlockSpec(memory_space=pltpu.VMEM)
    smem = pl.BlockSpec(memory_space=pltpu.SMEM)
    dma = pltpu.SemaphoreType.DMA
    shape = jax.ShapeDtypeStruct(coords.shape, F32)
    rows = lambda count, kind=F32: pltpu.VMEM((count, LANES), kind)
    edges = pltpu.VMEM((times, 4, 3 * HROW, LANES), F32)
    messages = pltpu.VMEM((times, DEVS, 1, LANES), F32)
    return pl.pallas_call(
        body,
        out_shape=(shape, shape),
        in_specs=[vmem] * 10 + [smem] * 3,
        out_specs=(vmem, vmem),
        scratch_shapes=[
            rows(3 * NROW),
            rows(3 * NROW),
            rows(3 * NROW),
            rows(3 * NROW),
            rows(EROW, I32),
            rows(IDXROW, I32),
            rows(IDXROW, I32),
            rows(3 * XROW),
            rows(12 * EROW),
            rows(12 * EROW),
            rows(3 * NROW),
            rows(3 * NROW),
            rows(12 * HROW),
            pltpu.VMEM(((IDXROW + SROW) // 2, 2 * LANES, LANES), BF16),
            pltpu.VMEM((CROW, DEVS, LANES), BF16),
            rows(CROW, I32),
            rows(2 * DEVS),
            rows(SROW, I32),
            rows(SROW, I32),
            rows(3 * SROW),
            rows(3 * SROW),
            rows(DEVS),
            edges,
            edges,
            edges,
            edges,
            messages,
            messages,
            dma((times, 4)),
            dma((times, 4)),
            dma((times, 4)),
            dma((times, 4)),
            dma((times,)),
            dma((times,)),
        ],
        compiler_params=pltpu.CompilerParams(
            collective_id=0, has_side_effects=True, vmem_limit_bytes=40 * 1024 * 1024
        ),
    )(
        coords,
        displacement,
        velocity,
        ext_force,
        elem_nodes,
        halo_lists,
        inv_mass.reshape(NROW, LANES),
        thickness.reshape(EROW, LANES),
        contact_nodes.reshape(CROW, LANES),
        contact_bucket.reshape(CROW, LANES),
        stiffness,
        block_class,
        tile_pairs,
    )


def solution(mesh):
    split = P(None, ("px", "py"))
    line = P(("px", "py"))
    placed = (
        split,
        split,
        split,
        line,
        split,
        line,
        P(),
        split,
        line,
        split,
        line,
        P(("px", "py"), None),
        split,
    )
    return jax.shard_map(
        device_step,
        mesh=mesh,
        in_specs=placed,
        out_specs=(split, split),
        check_vma=False,
    )
```

```python
import jax
import jax.numpy as jnp
from jax import lax
from jax.experimental import pallas as pl
from jax.experimental.pallas import tpu as pltpu
from jax.sharding import PartitionSpec as P

MESH = pl.DeviceIdType.MESH
LANES = 128
EBLK = 128
STEPS = 2
SUBS = 2
FAR = 10000.0
DT = 0.05
PENALTY = 0.5
REACH = 4.0

N_PX = 16
N_PY = 8
DEVS = N_PX * N_PY
NROW = 16
EROW = 16
HROW = 4
XROW = NROW + 4 * HROW
CROW = 16
SROW = 32
CAP = 32
PAIRS = 16
IDXROW = 4 * EROW + 4 * HROW
UNROLL = 4

F32 = jnp.float32
BF16 = jnp.bfloat16
I32 = jnp.int32


def iota(shape, dim):
    return lax.broadcasted_iota(I32, shape, dim)


def halves(value):
    upper = value.astype(BF16).astype(F32)
    return upper, value - upper


def gather(tables, place, rows, high, first, onehot, number, found, target, add):
    numbers = iota((NROW, LANES), 0) + place

    def some(step, carry):
        for inner in range(UNROLL):
            tile = step * UNROLL + inner
            both = jnp.dot(tables, onehot[number + tile], preferred_element_type=F32)
            for side in range(2):
                row = tile * 2 + side
                here = jnp.broadcast_to(high[pl.ds(first + row, 1), :], (NROW, LANES)) == numbers
                for c in range(3):
                    part = both[c * NROW : (c + 1) * NROW, side * LANES : (side + 1) * LANES]
                    total = jnp.sum(jnp.where(here, part, 0.0), axis=0, keepdims=True)
                    spot = pl.ds(target + c * rows + row, 1)
                    found[spot, :] = found[spot, :] + total if add else total
        return carry

    lax.fori_loop(0, rows // (2 * UNROLL), some, 0)


def split_table(table):
    return jnp.concatenate(halves(table), axis=1).astype(BF16)


def scatter(values, halved, rows, high, first, onehot, number, height):
    upper, lower = halves(values[pl.ds(0, 3 * rows), :])
    halved[pl.ds(0, 3 * rows), :] = upper
    halved[pl.ds(3 * rows, 3 * rows), :] = lower
    numbers = iota((16, LANES), 0).astype(F32).astype(BF16)

    def some(step, total):
        columns, right = [], []
        for inner in range(2 * UNROLL):
            row = step * 2 * UNROLL + inner
            mine = jnp.broadcast_to(high[pl.ds(first + row, 1), :], (16, LANES))
            mine = mine.astype(F32).astype(BF16)
            here = [mine == numbers + 16 * k for k in range(height // 16)]
            parts = []
            for part in range(6):
                value = jnp.broadcast_to(
                    halved[pl.ds(part * rows + row, 1), :], (16, LANES)
                ).astype(BF16)
                parts += [jnp.where(mask, value, jnp.zeros_like(value)) for mask in here]
            columns.append(jnp.concatenate(parts, axis=0))
        for inner in range(UNROLL):
            right.append(onehot[number + step * UNROLL + inner, pl.ds(0, LANES), :])
        return total + lax.dot_general(
            jnp.concatenate(columns, axis=1),
            jnp.concatenate(right, axis=1),
            (((1,), (1,)), ((), ())),
            preferred_element_type=F32,
        )

    total = lax.fori_loop(
        0, rows // (2 * UNROLL), some, jnp.zeros((6 * height, LANES), F32)
    )
    return total[: 3 * height] + total[3 * height :]


def build_onehots(low, first, rows, onehot, number):
    numbers = iota((LANES, LANES), 0)

    def some(step, carry):
        for inner in range(UNROLL):
            tile = step * UNROLL + inner
            for side in range(2):
                mine = low[pl.ds(first + tile * 2 + side, 1), :]
                here = jnp.broadcast_to(mine, (LANES, LANES)) == numbers
                ones = jnp.where(here, 1.0, 0.0).astype(BF16)
                for copy in range(2):
                    onehot[
                        number + tile,
                        pl.ds(copy * LANES, LANES),
                        pl.ds(side * LANES, LANES),
                    ] = ones
        return carry

    lax.fori_loop(0, rows // (2 * UNROLL), some, 0)


def body(
    coords_hbm,
    displacement_hbm,
    velocity_hbm,
    ext_force_hbm,
    elem_nodes_hbm,
    halo_lists_hbm,
    inv_mass_hbm,
    thickness_hbm,
    contact_nodes_hbm,
    bucket_hbm,
    stiffness_hbm,
    block_class_hbm,
    tile_pairs_hbm,
    disp_out,
    vel_out,
    coords,
    displacement,
    velocity,
    ext_force,
    elem_nodes,
    halo_lists,
    inv_mass,
    thickness,
    contact_nodes,
    bucket,
    stiffness,
    block_class,
    tile_pairs,
    base,
    disp,
    vel,
    fext,
    slow,
    spread,
    idx_low,
    idx_high,
    found,
    forces,
    held,
    halved,
    internal,
    contact,
    returned,
    ghosts,
    onehot,
    inverse,
    slot_low,
    slot_high,
    points,
    pushes,
    stage,
    halo_out,
    halo_in,
    back_out,
    back_in,
    slots_out,
    slots_in,
    loads,
    halo_sent,
    halo_got,
    back_sent,
    back_got,
    slots_sent,
    slots_got,
):
    sources = [
        bucket_hbm,
        contact_nodes_hbm,
        coords_hbm,
        displacement_hbm,
        halo_lists_hbm,
        elem_nodes_hbm,
        velocity_hbm,
        ext_force_hbm,
        inv_mass_hbm,
        thickness_hbm,
        stiffness_hbm,
        block_class_hbm,
        tile_pairs_hbm,
    ]
    targets = [
        bucket,
        contact_nodes,
        coords,
        displacement,
        halo_lists,
        elem_nodes,
        velocity,
        ext_force,
        inv_mass,
        thickness,
        stiffness,
        block_class,
        tile_pairs,
    ]
    copies = [
        pltpu.make_async_copy(source, target, loads.at[n])
        for n, (source, target) in enumerate(zip(sources, targets))
    ]
    for copy in copies:
        copy.start()

    i = lax.axis_index("px")
    j = lax.axis_index("py")
    me = i * N_PY + j
    neighbours = [
        (i > 0, (jnp.maximum(i - 1, 0), j)),
        (i < N_PX - 1, (jnp.minimum(i + 1, N_PX - 1), j)),
        (j > 0, (i, jnp.maximum(j - 1, 0))),
        (j < N_PY - 1, (i, jnp.minimum(j + 1, N_PY - 1))),
    ]
    facing = [1, 0, 3, 2]

    halo_in[...] = jnp.zeros_like(halo_in)
    back_in[...] = jnp.zeros_like(back_in)

    barrier = pltpu.get_barrier_semaphore()

    def greet(k, carry):
        other = lax.rem(me + k, DEVS)
        pl.semaphore_signal(
            barrier,
            inc=1,
            device_id=(other // N_PY, lax.rem(other, N_PY)),
            device_id_type=MESH,
        )
        return carry

    lax.fori_loop(1, DEVS, greet, 0)

    def to_rows(source, target, count, rows):
        for c in range(count):
            for r in range(rows):
                target[pl.ds(c * rows + r, 1), :] = source[
                    pl.ds(c, 1), pl.ds(r * LANES, LANES)
                ]

    devs = iota((LANES, LANES), 0)
    lanes = iota((LANES, LANES), 1)
    earlier = jnp.concatenate(
        [jnp.where(devs < lanes, 1.0, 0.0), jnp.ones((LANES, LANES), F32)], axis=1
    ).astype(BF16)
    copies[0].wait()
    before = jnp.zeros((LANES, LANES), F32)
    named, ranks = [], []
    for row in range(CROW):
        here = jnp.broadcast_to(bucket[pl.ds(row, 1), :], (LANES, LANES)) == devs
        ones = jnp.where(here, 1.0, 0.0).astype(BF16)
        counts = jnp.dot(ones, earlier, preferred_element_type=F32)
        ranks.append(
            jnp.sum(jnp.where(here, counts[:, :LANES] + before, 0.0), axis=0, keepdims=True)
        )
        before = before + counts[:, LANES:]
        named.append(ones)

    copies[1].wait()
    slot_row = (devs & (CAP - 1)).astype(F32)
    nodes = jnp.zeros((LANES, 2 * LANES), F32)
    for row in range(0, CROW, 2):
        right = []
        for one in (row, row + 1):
            here = jnp.broadcast_to(ranks[one], (LANES, LANES)) == slot_row
            node = contact_nodes[pl.ds(one, 1), :]
            low = jnp.broadcast_to((node & (LANES - 1)).astype(F32), (LANES, LANES))
            high = jnp.broadcast_to(((node >> 7) + 1).astype(F32), (LANES, LANES))
            right.append(
                jnp.concatenate(
                    [jnp.where(here, low, 0.0), jnp.where(here, high, 0.0)], axis=0
                ).astype(BF16)
            )
        nodes = nodes + lax.dot_general(
            jnp.concatenate([named[row], named[row + 1]], axis=1),
            jnp.concatenate(right, axis=1),
            (((1,), (1,)), ((), ())),
            preferred_element_type=F32,
        )
    inverse[pl.ds(0, DEVS), :] = nodes[:, :LANES]
    inverse[pl.ds(DEVS, DEVS), :] = nodes[:, LANES:]
    block = iota((SROW, LANES), 1) >> 5
    low = jnp.zeros((SROW, LANES), F32)
    high = jnp.zeros((SROW, LANES), F32)
    for q in range(4):
        low = jnp.where(block == q, inverse[pl.ds(q, SROW, stride=4), :], low)
        high = jnp.where(block == q, inverse[pl.ds(DEVS + q, SROW, stride=4), :], high)
    slot_low[...] = low.astype(I32)
    slot_high[...] = high.astype(I32) - 1
    build_onehots(slot_low, 0, SROW, onehot, IDXROW // 2)

    copies[2].wait()
    copies[3].wait()
    to_rows(coords, base, 3, NROW)
    to_rows(displacement, disp, 3, NROW)

    def prepare_halo():
        copies[4].wait()
        for k in range(4):
            for r in range(HROW):
                entry = halo_lists[pl.ds(k, 1), pl.ds(r * LANES, LANES)]
                idx_low[pl.ds(4 * EROW + k * HROW + r, 1), :] = entry & (LANES - 1)
                idx_high[pl.ds(4 * EROW + k * HROW + r, 1), :] = entry >> 7
        build_onehots(idx_low, 4 * EROW, 4 * HROW, onehot, 2 * EROW)

    def prepare_rest():
        for copy in copies[5:]:
            copy.wait()
        for k in range(4):
            for r in range(EROW):
                entry = elem_nodes[pl.ds(k, 1), pl.ds(r * LANES, LANES)]
                idx_low[pl.ds(k * EROW + r, 1), :] = entry & (LANES - 1)
                idx_high[pl.ds(k * EROW + r, 1), :] = entry >> 7
        build_onehots(idx_low, 0, 4 * EROW, onehot, 0)
        to_rows(velocity, vel, 3, NROW)
        to_rows(ext_force, fext, 3, NROW)
        for r in range(EROW):
            slow[pl.ds(r, 1), :] = jnp.full((1, LANES), block_class[r], I32)
        for column in range(12):
            spread[pl.ds(column * 16, 12), :] = jnp.broadcast_to(
                stiffness[:, column : column + 1], (12, LANES)
            )

    def exchange_start(number, source, target, sent, got):
        for n, (exists, device) in enumerate(neighbours):

            @pl.when(exists)
            def _():
                pltpu.make_async_remote_copy(
                    src_ref=source.at[number, n],
                    dst_ref=target.at[number, facing[n]],
                    send_sem=sent.at[number, n],
                    recv_sem=got.at[number, facing[n]],
                    device_id=device,
                    device_id_type=MESH,
                ).start()

    def exchange_wait(number, buffer, sem):
        for n, (exists, _unused) in enumerate(neighbours):

            @pl.when(exists)
            def _():
                pltpu.make_async_copy(
                    buffer.at[number, n], buffer.at[number, n], sem.at[number, n]
                ).wait()

    def slots_start(number):
        def send(k, carry):
            other = lax.rem(me + k, DEVS)
            pltpu.make_async_remote_copy(
                src_ref=slots_out.at[number, other],
                dst_ref=slots_in.at[number, me],
                send_sem=slots_sent.at[number],
                recv_sem=slots_got.at[number],
                device_id=(other // N_PY, lax.rem(other, N_PY)),
                device_id_type=MESH,
            ).start()
            return carry

        lax.fori_loop(1, DEVS, send, 0)
        slots_in[number, me] = slots_out[number, me]

    def slots_wait(number, buffer, sem):
        part = buffer.at[number, pl.ds(0, DEVS - 1)]
        pltpu.make_async_copy(part, part, sem.at[number]).wait()

    def to_messages(parts, number):
        for q in range(4):
            mixed = jnp.zeros((SROW, LANES), F32)
            for c in range(3):
                shift = (CAP * (c - q)) % LANES
                turned = pltpu.roll(parts[c], shift, 1) if shift else parts[c]
                mixed = jnp.where(block == c, turned, mixed)
            stage[pl.ds(q * SROW, SROW), :] = mixed
        for a in range(SROW):
            for q in range(4):
                slots_out[number, 4 * a + q] = stage[pl.ds(q * SROW + a, 1), :]

    def from_messages(number):
        for a in range(SROW):
            for q in range(4):
                stage[pl.ds(q * SROW + a, 1), :] = slots_in[number, 4 * a + q]
        parts = []
        for c in range(3):
            mixed = jnp.zeros((SROW, LANES), F32)
            for q in range(4):
                shift = (CAP * (q - c)) % LANES
                rows = stage[pl.ds(q * SROW, SROW), :]
                turned = pltpu.roll(rows, shift, 1) if shift else rows
                mixed = jnp.where(block == q, turned, mixed)
            parts.append(mixed)
        return parts

    def send_points(number):
        gather(
            split_table(base[...] + disp[...]),
            0,
            SROW,
            slot_high,
            0,
            onehot,
            IDXROW // 2,
            points,
            0,
            False,
        )
        empty = slot_high[...] < 0
        to_messages(
            [jnp.where(empty, FAR, points[pl.ds(c * SROW, SROW), :]) for c in range(3)],
            number,
        )

    def push_tiles(number):
        for c, part in enumerate(from_messages(number)):
            points[pl.ds(c * SROW, SROW), :] = part
        numbers = iota((SROW, LANES), 0)

        def one_pair(p, totals):
            first = tile_pairs[0, p]
            second = tile_pairs[1, p]
            mine = [
                jnp.broadcast_to(points[pl.ds(c * SROW + first, 1), :], (8, LANES))
                for c in range(3)
            ]
            others = [
                jnp.broadcast_to(points[pl.ds(c * SROW + second, 1), :], (8, LANES))
                for c in range(3)
            ]
            sums = [jnp.zeros((8, LANES), F32) for c in range(3)]
            for turn in range(LANES // 8):
                gap = [
                    mine[c] - pltpu.roll(others[c], turn * 8, 1, stride=1, stride_axis=0)
                    for c in range(3)
                ]
                dist = gap[0] * gap[0] + gap[1] * gap[1] + gap[2] * gap[2]
                weight = PENALTY * jnp.exp(dist * (-1.0 / REACH))
                sums = [sums[c] + weight * gap[c] for c in range(3)]
            return tuple(
                totals[c]
                + jnp.where(numbers == first, jnp.sum(sums[c], axis=0, keepdims=True), 0.0)
                for c in range(3)
            )

        zero = jnp.zeros((SROW, LANES), F32)
        return lax.fori_loop(0, PAIRS, one_pair, (zero, zero, zero))

    def send_edges(number):
        gather(
            split_table(disp[...]),
            0,
            4 * HROW,
            idx_high,
            4 * EROW,
            onehot,
            2 * EROW,
            returned,
            0,
            False,
        )
        for n in range(4):
            for c in range(3):
                halo_out[number, n, pl.ds(c * HROW, HROW), :] = returned[
                    pl.ds((c * 4 + n) * HROW, HROW), :
                ]
        exchange_start(number, halo_out, halo_in, halo_sent, halo_got)

    def own_corners():
        gather(
            split_table(disp[...]), 0, 4 * EROW, idx_high, 0, onehot, 0, found, 0, False
        )

    def element_stage(number, sub_no):
        exchange_wait(number, halo_in, halo_got)
        for n in range(4):
            for c in range(3):
                ghosts[pl.ds((c * 4 + n) * HROW, HROW), :] = halo_in[
                    number, n, pl.ds(c * HROW, HROW), :
                ]
        gather(
            split_table(ghosts[...]), NROW, 4 * EROW, idx_high, 0, onehot, 0, found, 0, True
        )
        local = [found[pl.ds(n * EROW, EROW), :] for n in range(12)]
        thick = thickness[...]
        for out in range(12):
            total = jnp.zeros((EROW, LANES), F32)
            for of in range(12):
                factor = spread[pl.ds(of * 16 + out, 1), :]
                total = total + jnp.broadcast_to(factor, (EROW, LANES)) * local[of]
            total = thick * total
            place = pl.ds(out * EROW, EROW)
            if sub_no == 0:
                held[place, :] = total
            else:
                total = jnp.where(slow[...] == 1, held[place, :], total)
            forces[place, :] = total
        summed = scatter(forces, halved, 4 * EROW, idx_high, 0, onehot, 0, XROW)
        for c in range(3):
            internal[pl.ds(c * NROW, NROW), :] = summed[c * XROW : c * XROW + NROW]
            for n in range(4):
                first = c * XROW + NROW + n * HROW
                back_out[number, n, pl.ds(c * HROW, HROW), :] = summed[first : first + HROW]
        exchange_start(number, back_out, back_in, back_sent, back_got)

    def return_stage(number):
        exchange_wait(number, back_in, back_got)
        for n in range(4):
            for c in range(3):
                returned[pl.ds(c * 4 * HROW + n * HROW, HROW), :] = back_in[
                    number, n, pl.ds(c * HROW, HROW), :
                ]
        internal[...] = internal[...] + scatter(
            returned, halved, 4 * HROW, idx_high, 4 * EROW, onehot, 2 * EROW, NROW
        )

    def update():
        mass = inv_mass[...]
        for c in range(3):
            place = pl.ds(c * NROW, NROW)
            accel = mass * (fext[place, :] - internal[place, :] + contact[place, :])
            speed = vel[place, :] + DT * accel
            vel[place, :] = speed
            disp[place, :] = disp[place, :] + DT * speed

    def major(step, carry):
        there, back = 2 * step, 2 * step + 1
        send_points(there)

        @pl.when(step == 0)
        def _():
            pl.semaphore_wait(barrier, DEVS - 1)

        slots_start(there)
        pl.when(step == 0)(prepare_halo)
        send_edges(there)
        pl.when(step == 0)(prepare_rest)
        own_corners()
        element_stage(there, 0)
        slots_wait(there, slots_in, slots_got)
        to_messages(push_tiles(there), back)
        slots_start(back)
        return_stage(there)
        slots_wait(back, slots_in, slots_got)
        for c, part in enumerate(from_messages(back)):
            pushes[pl.ds(c * SROW, SROW), :] = part
        contact[...] = scatter(
            pushes, halved, SROW, slot_high, 0, onehot, IDXROW // 2, NROW
        )
        update()
        for sub_no in range(1, SUBS):
            send_edges(back)
            own_corners()
            element_stage(back, sub_no)
            return_stage(back)
            update()
        return carry

    lax.fori_loop(0, STEPS, major, 0)

    for c in range(3):
        for r in range(NROW):
            row = pl.ds(c * NROW + r, 1)
            place = pl.ds(r * LANES, LANES)
            disp_out[pl.ds(c, 1), place] = disp[row, :]
            vel_out[pl.ds(c, 1), place] = vel[row, :]

    def drain(number, carry):
        exchange_wait(number, halo_out, halo_sent)
        exchange_wait(number, back_out, back_sent)
        slots_wait(number, slots_out, slots_sent)
        return carry

    lax.fori_loop(0, STEPS * SUBS, drain, 0)


def device_step(
    coords,
    displacement,
    velocity,
    inv_mass,
    ext_force,
    thickness,
    stiffness,
    elem_nodes,
    block_class,
    halo_lists,
    contact_nodes,
    contact_bucket,
    tile_pairs,
):
    times = STEPS * SUBS
    vmem = pl.BlockSpec(memory_space=pltpu.VMEM)
    apart = pl.BlockSpec(memory_space=pltpu.HBM)
    dma = pltpu.SemaphoreType.DMA
    shape = jax.ShapeDtypeStruct(coords.shape, F32)
    rows = lambda count, kind=F32: pltpu.VMEM((count, LANES), kind)
    field = pltpu.VMEM(coords.shape, F32)
    edges = pltpu.VMEM((times, 4, 3 * HROW, LANES), F32)
    messages = pltpu.VMEM((times, DEVS, 1, LANES), F32)
    return pl.pallas_call(
        body,
        out_shape=(shape, shape),
        in_specs=[apart] * 13,
        out_specs=(vmem, vmem),
        scratch_shapes=[
            field,
            field,
            field,
            field,
            pltpu.VMEM(elem_nodes.shape, I32),
            pltpu.VMEM(halo_lists.shape, I32),
            rows(NROW),
            rows(EROW),
            rows(CROW, I32),
            rows(CROW, I32),
            pltpu.VMEM(stiffness.shape, F32),
            pltpu.SMEM(block_class.shape, I32),
            pltpu.SMEM(tile_pairs.shape, I32),
            rows(3 * NROW),
            rows(3 * NROW),
            rows(3 * NROW),
            rows(3 * NROW),
            rows(EROW, I32),
            rows(12 * 16),
            rows(IDXROW, I32),
            rows(IDXROW, I32),
            rows(12 * EROW),
            rows(12 * EROW),
            rows(12 * EROW),
            rows(24 * EROW),
            rows(3 * NROW),
            rows(3 * NROW),
            rows(12 * HROW),
            rows(12 * HROW),
            pltpu.VMEM(((IDXROW + SROW) // 2, 2 * LANES, 2 * LANES), BF16),
            rows(2 * DEVS),
            rows(SROW, I32),
            rows(SROW, I32),
            rows(3 * SROW),
            rows(3 * SROW),
            rows(DEVS),
            edges,
            edges,
            edges,
            edges,
            messages,
            messages,
            dma((13,)),
            dma((times, 4)),
            dma((times, 4)),
            dma((times, 4)),
            dma((times, 4)),
            dma((times,)),
            dma((times,)),
        ],
        compiler_params=pltpu.CompilerParams(
            collective_id=0, has_side_effects=True, vmem_limit_bytes=60 * 1024 * 1024
        ),
    )(
        coords,
        displacement,
        velocity,
        ext_force,
        elem_nodes,
        halo_lists,
        inv_mass.reshape(NROW, LANES),
        thickness.reshape(EROW, LANES),
        contact_nodes.reshape(CROW, LANES),
        contact_bucket.reshape(CROW, LANES),
        stiffness,
        block_class,
        tile_pairs,
    )


def solution(mesh):
    split = P(None, ("px", "py"))
    line = P(("px", "py"))
    placed = (
        split,
        split,
        split,
        line,
        split,
        line,
        P(),
        split,
        line,
        split,
        line,
        P(("px", "py"), None),
        split,
    )
    return jax.shard_map(
        device_step,
        mesh=mesh,
        in_specs=placed,
        out_specs=(split, split),
        check_vma=False,
    )
```

```python
import jax
import jax.numpy as jnp
from jax import lax
from jax.experimental import pallas as pl
from jax.experimental.pallas import tpu as pltpu
from jax.sharding import PartitionSpec as P

MESH = pl.DeviceIdType.MESH
LANES = 128
EBLK = 128
STEPS = 2
SUBS = 2
FAR = 10000.0
DT = 0.05
PENALTY = 0.5
REACH = 4.0

N_PX = 16
N_PY = 8
DEVS = N_PX * N_PY
NROW = 16
EROW = 16
HROW = 4
XROW = NROW + 4 * HROW
CROW = 16
SROW = 32
CAP = 32
PAIRS = 16
IDXROW = 4 * EROW + 4 * HROW
UNROLL = 16
PAIR_UNROLL = 4

F32 = jnp.float32
BF16 = jnp.bfloat16
I32 = jnp.int32


def iota(shape, dim):
    return lax.broadcasted_iota(I32, shape, dim)


def halves(value):
    upper = value.astype(BF16).astype(F32)
    return upper, value - upper


def gather(tables, place, rows, high, first, onehot, number, found, target, add):
    unroll = min(UNROLL, rows // 2)
    numbers = iota((NROW, LANES), 0) + place

    def some(step, carry):
        for inner in range(unroll):
            tile = step * unroll + inner
            both = jnp.dot(
                tables, onehot[number + tile], preferred_element_type=F32
            )
            for side in range(2):
                row = tile * 2 + side
                here = jnp.broadcast_to(high[pl.ds(first + row, 1), :], (NROW, LANES)) == numbers
                lane = slice(side * LANES, (side + 1) * LANES)
                for c in range(3):
                    upper = both[c * NROW : (c + 1) * NROW, lane]
                    part = upper + both[(c + 3) * NROW : (c + 4) * NROW, lane]
                    total = jnp.sum(jnp.where(here, part, 0.0), axis=0, keepdims=True)
                    spot = pl.ds(target + c * rows + row, 1)
                    found[spot, :] = found[spot, :] + total if add else total
        return carry

    lax.fori_loop(0, rows // (2 * unroll), some, 0)


def split_table(table):
    return jnp.concatenate(halves(table), axis=0).astype(BF16)


def scatter(values, halved, rows, high, first, onehot, number, height):
    unroll = min(UNROLL, rows // 2)
    upper, lower = halves(values[pl.ds(0, 3 * rows), :])
    halved[pl.ds(0, 3 * rows), :] = upper
    halved[pl.ds(3 * rows, 3 * rows), :] = lower
    numbers = iota((16, LANES), 0).astype(F32).astype(BF16)

    def some(step, total):
        columns, right = [], []
        for inner in range(2 * unroll):
            row = step * 2 * unroll + inner
            mine = jnp.broadcast_to(high[pl.ds(first + row, 1), :], (16, LANES))
            mine = mine.astype(F32).astype(BF16)
            here = [mine == numbers + 16 * k for k in range(height // 16)]
            parts = []
            for part in range(6):
                value = jnp.broadcast_to(
                    halved[pl.ds(part * rows + row, 1), :], (16, LANES)
                ).astype(BF16)
                parts += [jnp.where(mask, value, jnp.zeros_like(value)) for mask in here]
            columns.append(jnp.concatenate(parts, axis=0))
        for inner in range(unroll):
            right.append(onehot[number + step * unroll + inner])
        return total + lax.dot_general(
            jnp.concatenate(columns, axis=1),
            jnp.concatenate(right, axis=1),
            (((1,), (1,)), ((), ())),
            preferred_element_type=F32,
        )

    total = lax.fori_loop(
        0, rows // (2 * unroll), some, jnp.zeros((6 * height, LANES), F32)
    )
    return total[: 3 * height] + total[3 * height :]


def build_onehots(low, first, rows, onehot, number):
    unroll = min(UNROLL, rows // 2)
    numbers = iota((LANES, LANES), 0)

    def some(step, carry):
        for inner in range(unroll):
            tile = step * unroll + inner
            for side in range(2):
                mine = low[pl.ds(first + tile * 2 + side, 1), :]
                here = jnp.broadcast_to(mine, (LANES, LANES)) == numbers
                ones = jnp.where(here, 1.0, 0.0).astype(BF16)
                onehot[number + tile, :, pl.ds(side * LANES, LANES)] = ones
        return carry

    lax.fori_loop(0, rows // (2 * unroll), some, 0)


def body(
    coords_hbm,
    displacement_hbm,
    velocity_hbm,
    ext_force_hbm,
    elem_nodes_hbm,
    halo_lists_hbm,
    inv_mass_hbm,
    thickness_hbm,
    contact_nodes_hbm,
    bucket_hbm,
    stiffness_hbm,
    block_class_hbm,
    tile_pairs_hbm,
    disp_out,
    vel_out,
    coords,
    displacement,
    velocity,
    ext_force,
    elem_nodes,
    halo_lists,
    inv_mass,
    thickness,
    contact_nodes,
    bucket,
    stiffness,
    block_class,
    tile_pairs,
    base,
    disp,
    vel,
    fext,
    slow,
    spread,
    idx_low,
    idx_high,
    found,
    forces,
    held,
    halved,
    internal,
    contact,
    returned,
    ghosts,
    onehot,
    inverse,
    slot_low,
    slot_high,
    points,
    pushes,
    stage,
    halo_out,
    halo_in,
    back_out,
    back_in,
    slots_out,
    slots_in,
    loads,
    halo_sent,
    halo_got,
    back_sent,
    back_got,
    slots_sent,
    slots_got,
):
    sources = [
        bucket_hbm,
        contact_nodes_hbm,
        coords_hbm,
        displacement_hbm,
        halo_lists_hbm,
        elem_nodes_hbm,
        velocity_hbm,
        ext_force_hbm,
        inv_mass_hbm,
        thickness_hbm,
        stiffness_hbm,
        block_class_hbm,
        tile_pairs_hbm,
    ]
    targets = [
        bucket,
        contact_nodes,
        coords,
        displacement,
        halo_lists,
        elem_nodes,
        velocity,
        ext_force,
        inv_mass,
        thickness,
        stiffness,
        block_class,
        tile_pairs,
    ]
    copies = [
        pltpu.make_async_copy(source, target, loads.at[n])
        for n, (source, target) in enumerate(zip(sources, targets))
    ]
    for copy in copies:
        copy.start()

    i = lax.axis_index("px")
    j = lax.axis_index("py")
    me = i * N_PY + j
    neighbours = [
        (i > 0, (jnp.maximum(i - 1, 0), j)),
        (i < N_PX - 1, (jnp.minimum(i + 1, N_PX - 1), j)),
        (j > 0, (i, jnp.maximum(j - 1, 0))),
        (j < N_PY - 1, (i, jnp.minimum(j + 1, N_PY - 1))),
    ]
    facing = [1, 0, 3, 2]

    halo_in[...] = jnp.zeros_like(halo_in)
    back_in[...] = jnp.zeros_like(back_in)

    barrier = pltpu.get_barrier_semaphore()

    flips = [
        j + sum((1 - 2 * lax.rem(j // (1 << b), 2)) * (1 << b) for b in range(3) if mask >> b & 1)
        for mask in range(N_PY)
    ]

    def flip(mask):
        return sum(lax.rem(i // (1 << b) + mask // (1 << b), 2) * (1 << b) for b in range(4))

    def everyone(act):
        def some(step, carry):
            px = flip(N_PX - 1 - step)
            for py in flips[::-1]:
                act(px, py)
            return carry

        lax.fori_loop(0, N_PX - 1, some, 0)
        for py in flips[:0:-1]:
            act(i, py)

    def greet(px, py):
        pl.semaphore_signal(barrier, inc=1, device_id=(px, py), device_id_type=MESH)

    everyone(greet)

    def to_rows(source, target, count, rows):
        for c in range(count):
            for r in range(rows):
                target[pl.ds(c * rows + r, 1), :] = source[
                    pl.ds(c, 1), pl.ds(r * LANES, LANES)
                ]

    devs = iota((LANES, LANES), 0)
    lanes = iota((LANES, LANES), 1)
    earlier = jnp.concatenate(
        [jnp.where(devs < lanes, 1.0, 0.0), jnp.ones((LANES, LANES), F32)], axis=1
    ).astype(BF16)
    copies[0].wait()
    before = jnp.zeros((LANES, LANES), F32)
    named, ranks = [], []
    for row in range(CROW):
        here = jnp.broadcast_to(bucket[pl.ds(row, 1), :], (LANES, LANES)) == devs
        ones = jnp.where(here, 1.0, 0.0).astype(BF16)
        counts = jnp.dot(ones, earlier, preferred_element_type=F32)
        ranks.append(
            jnp.sum(jnp.where(here, counts[:, :LANES] + before, 0.0), axis=0, keepdims=True)
        )
        before = before + counts[:, LANES:]
        named.append(ones)

    copies[1].wait()
    slot_row = (devs & (CAP - 1)).astype(F32)
    nodes = jnp.zeros((LANES, 2 * LANES), F32)
    for row in range(0, CROW, 2):
        right = []
        for one in (row, row + 1):
            here = jnp.broadcast_to(ranks[one], (LANES, LANES)) == slot_row
            node = contact_nodes[pl.ds(one, 1), :]
            low = jnp.broadcast_to((node & (LANES - 1)).astype(F32), (LANES, LANES))
            high = jnp.broadcast_to(((node >> 7) + 1).astype(F32), (LANES, LANES))
            right.append(
                jnp.concatenate(
                    [jnp.where(here, low, 0.0), jnp.where(here, high, 0.0)], axis=0
                ).astype(BF16)
            )
        nodes = nodes + lax.dot_general(
            jnp.concatenate([named[row], named[row + 1]], axis=1),
            jnp.concatenate(right, axis=1),
            (((1,), (1,)), ((), ())),
            preferred_element_type=F32,
        )
    inverse[pl.ds(0, DEVS), :] = nodes[:, :LANES]
    inverse[pl.ds(DEVS, DEVS), :] = nodes[:, LANES:]
    block = iota((SROW, LANES), 1) >> 5
    low = jnp.zeros((SROW, LANES), F32)
    high = jnp.zeros((SROW, LANES), F32)
    for q in range(4):
        low = jnp.where(block == q, inverse[pl.ds(q, SROW, stride=4), :], low)
        high = jnp.where(block == q, inverse[pl.ds(DEVS + q, SROW, stride=4), :], high)
    slot_low[...] = low.astype(I32)
    slot_high[...] = high.astype(I32) - 1
    build_onehots(slot_low, 0, SROW, onehot, IDXROW // 2)

    copies[2].wait()
    copies[3].wait()
    to_rows(coords, base, 3, NROW)
    to_rows(displacement, disp, 3, NROW)

    def prepare_halo():
        copies[4].wait()
        for k in range(4):
            for r in range(HROW):
                entry = halo_lists[pl.ds(k, 1), pl.ds(r * LANES, LANES)]
                idx_low[pl.ds(4 * EROW + k * HROW + r, 1), :] = entry & (LANES - 1)
                idx_high[pl.ds(4 * EROW + k * HROW + r, 1), :] = entry >> 7
        build_onehots(idx_low, 4 * EROW, 4 * HROW, onehot, 2 * EROW)

    def prepare_rest():
        for copy in copies[5:]:
            copy.wait()
        for k in range(4):
            for r in range(EROW):
                entry = elem_nodes[pl.ds(k, 1), pl.ds(r * LANES, LANES)]
                idx_low[pl.ds(k * EROW + r, 1), :] = entry & (LANES - 1)
                idx_high[pl.ds(k * EROW + r, 1), :] = entry >> 7
        build_onehots(idx_low, 0, 4 * EROW, onehot, 0)
        to_rows(velocity, vel, 3, NROW)
        to_rows(ext_force, fext, 3, NROW)
        for r in range(EROW):
            slow[pl.ds(r, 1), :] = jnp.full((1, LANES), block_class[r], I32)
        for column in range(12):
            spread[pl.ds(column * 16, 12), :] = jnp.broadcast_to(
                stiffness[:, column : column + 1], (12, LANES)
            )

    def exchange_start(number, source, target, sent, got):
        for n, (exists, device) in enumerate(neighbours):

            @pl.when(exists)
            def _():
                pltpu.make_async_remote_copy(
                    src_ref=source.at[number, n],
                    dst_ref=target.at[number, facing[n]],
                    send_sem=sent.at[number, n],
                    recv_sem=got.at[number, facing[n]],
                    device_id=device,
                    device_id_type=MESH,
                ).start()

    def exchange_wait(number, buffer, sem):
        for n, (exists, _unused) in enumerate(neighbours):

            @pl.when(exists)
            def _():
                pltpu.make_async_copy(
                    buffer.at[number, n], buffer.at[number, n], sem.at[number, n]
                ).wait()

    def slots_start(number):
        def send(px, py):
            pltpu.make_async_remote_copy(
                src_ref=slots_out.at[number, px * N_PY + py],
                dst_ref=slots_in.at[number, me],
                send_sem=slots_sent.at[number],
                recv_sem=slots_got.at[number],
                device_id=(px, py),
                device_id_type=MESH,
            ).start()

        everyone(send)
        slots_in[number, me] = slots_out[number, me]

    def slots_wait(number, buffer, sem):
        part = buffer.at[number, pl.ds(0, DEVS - 1)]
        pltpu.make_async_copy(part, part, sem.at[number]).wait()

    def to_messages(parts, number):
        for q in range(4):
            mixed = jnp.zeros((SROW, LANES), F32)
            for c in range(3):
                shift = (CAP * (c - q)) % LANES
                turned = pltpu.roll(parts[c], shift, 1) if shift else parts[c]
                mixed = jnp.where(block == c, turned, mixed)
            stage[pl.ds(q * SROW, SROW), :] = mixed
        for a in range(SROW):
            for q in range(4):
                slots_out[number, 4 * a + q] = stage[pl.ds(q * SROW + a, 1), :]

    def from_messages(number):
        for a in range(SROW):
            for q in range(4):
                stage[pl.ds(q * SROW + a, 1), :] = slots_in[number, 4 * a + q]
        parts = []
        for c in range(3):
            mixed = jnp.zeros((SROW, LANES), F32)
            for q in range(4):
                shift = (CAP * (q - c)) % LANES
                rows = stage[pl.ds(q * SROW, SROW), :]
                turned = pltpu.roll(rows, shift, 1) if shift else rows
                mixed = jnp.where(block == q, turned, mixed)
            parts.append(mixed)
        return parts

    def send_points(number):
        gather(
            split_table(base[...] + disp[...]),
            0,
            SROW,
            slot_high,
            0,
            onehot,
            IDXROW // 2,
            points,
            0,
            False,
        )
        empty = slot_high[...] < 0
        to_messages(
            [jnp.where(empty, FAR, points[pl.ds(c * SROW, SROW), :]) for c in range(3)],
            number,
        )

    def push_tiles(number):
        for c, part in enumerate(from_messages(number)):
            points[pl.ds(c * SROW, SROW), :] = part
        numbers = iota((SROW, LANES), 0)

        def some_pairs(step, totals):
            for inner in range(PAIR_UNROLL):
                totals = one_pair(step * PAIR_UNROLL + inner, totals)
            return totals

        def one_pair(p, totals):
            first = tile_pairs[0, p]
            second = tile_pairs[1, p]
            mine = [
                jnp.broadcast_to(points[pl.ds(c * SROW + first, 1), :], (8, LANES))
                for c in range(3)
            ]
            others = [
                jnp.broadcast_to(points[pl.ds(c * SROW + second, 1), :], (8, LANES))
                for c in range(3)
            ]
            sums = [jnp.zeros((8, LANES), F32) for c in range(3)]
            for turn in range(LANES // 8):
                gap = [
                    mine[c] - pltpu.roll(others[c], turn * 8, 1, stride=1, stride_axis=0)
                    for c in range(3)
                ]
                dist = gap[0] * gap[0] + gap[1] * gap[1] + gap[2] * gap[2]
                weight = PENALTY * jnp.exp(dist * (-1.0 / REACH))
                sums = [sums[c] + weight * gap[c] for c in range(3)]
            return tuple(
                totals[c]
                + jnp.where(numbers == first, jnp.sum(sums[c], axis=0, keepdims=True), 0.0)
                for c in range(3)
            )

        zero = jnp.zeros((SROW, LANES), F32)
        return lax.fori_loop(0, PAIRS // PAIR_UNROLL, some_pairs, (zero, zero, zero))

    def list_edges(number):
        gather(
            split_table(disp[...]),
            0,
            4 * HROW,
            idx_high,
            4 * EROW,
            onehot,
            2 * EROW,
            returned,
            0,
            False,
        )
        for n in range(4):
            for c in range(3):
                halo_out[number, n, pl.ds(c * HROW, HROW), :] = returned[
                    pl.ds((c * 4 + n) * HROW, HROW), :
                ]

    def send_edges(number):
        exchange_start(number, halo_out, halo_in, halo_sent, halo_got)

    def own_corners():
        gather(
            split_table(disp[...]), 0, 4 * EROW, idx_high, 0, onehot, 0, found, 0, False
        )

    def element_stage(number, sub_no):
        exchange_wait(number, halo_in, halo_got)
        for n in range(4):
            for c in range(3):
                ghosts[pl.ds((c * 4 + n) * HROW, HROW), :] = halo_in[
                    number, n, pl.ds(c * HROW, HROW), :
                ]
        gather(
            split_table(ghosts[...]), NROW, 4 * EROW, idx_high, 0, onehot, 0, found, 0, True
        )
        local = [found[pl.ds(n * EROW, EROW), :] for n in range(12)]
        thick = thickness[...]
        for out in range(12):
            total = jnp.zeros((EROW, LANES), F32)
            for of in range(12):
                factor = spread[pl.ds(of * 16 + out, 1), :]
                total = total + jnp.broadcast_to(factor, (EROW, LANES)) * local[of]
            total = thick * total
            place = pl.ds(out * EROW, EROW)
            if sub_no == 0:
                held[place, :] = total
            else:
                total = jnp.where(slow[...] == 1, held[place, :], total)
            forces[place, :] = total
        summed = scatter(forces, halved, 4 * EROW, idx_high, 0, onehot, 0, XROW)
        for c in range(3):
            internal[pl.ds(c * NROW, NROW), :] = summed[c * XROW : c * XROW + NROW]
            for n in range(4):
                first = c * XROW + NROW + n * HROW
                back_out[number, n, pl.ds(c * HROW, HROW), :] = summed[first : first + HROW]
        exchange_start(number, back_out, back_in, back_sent, back_got)

    def return_stage(number):
        exchange_wait(number, back_in, back_got)
        for n in range(4):
            for c in range(3):
                returned[pl.ds(c * 4 * HROW + n * HROW, HROW), :] = back_in[
                    number, n, pl.ds(c * HROW, HROW), :
                ]
        internal[...] = internal[...] + scatter(
            returned, halved, 4 * HROW, idx_high, 4 * EROW, onehot, 2 * EROW, NROW
        )

    def update():
        mass = inv_mass[...]
        for c in range(3):
            place = pl.ds(c * NROW, NROW)
            accel = mass * (fext[place, :] - internal[place, :] + contact[place, :])
            speed = vel[place, :] + DT * accel
            vel[place, :] = speed
            disp[place, :] = disp[place, :] + DT * speed

    def major(step, carry):
        there, back = 2 * step, 2 * step + 1
        pl.when(step == 0)(prepare_halo)
        list_edges(there)
        send_points(there)

        @pl.when(step == 0)
        def _():
            pl.semaphore_wait(barrier, DEVS - 1)

        send_edges(there)
        slots_start(there)
        pl.when(step == 0)(prepare_rest)
        own_corners()
        element_stage(there, 0)
        slots_wait(there, slots_in, slots_got)
        to_messages(push_tiles(there), back)
        slots_start(back)
        return_stage(there)
        slots_wait(back, slots_in, slots_got)
        for c, part in enumerate(from_messages(back)):
            pushes[pl.ds(c * SROW, SROW), :] = part
        contact[...] = scatter(
            pushes, halved, SROW, slot_high, 0, onehot, IDXROW // 2, NROW
        )
        update()
        for sub_no in range(1, SUBS):
            list_edges(back)
            send_edges(back)
            own_corners()
            element_stage(back, sub_no)
            return_stage(back)
            update()
        return carry

    lax.fori_loop(0, STEPS, major, 0)

    for c in range(3):
        for r in range(NROW):
            row = pl.ds(c * NROW + r, 1)
            place = pl.ds(r * LANES, LANES)
            disp_out[pl.ds(c, 1), place] = disp[row, :]
            vel_out[pl.ds(c, 1), place] = vel[row, :]

    def drain(number, carry):
        exchange_wait(number, halo_out, halo_sent)
        exchange_wait(number, back_out, back_sent)
        slots_wait(number, slots_out, slots_sent)
        return carry

    lax.fori_loop(0, STEPS * SUBS, drain, 0)


def device_step(
    coords,
    displacement,
    velocity,
    inv_mass,
    ext_force,
    thickness,
    stiffness,
    elem_nodes,
    block_class,
    halo_lists,
    contact_nodes,
    contact_bucket,
    tile_pairs,
):
    times = STEPS * SUBS
    vmem = pl.BlockSpec(memory_space=pltpu.VMEM)
    apart = pl.BlockSpec(memory_space=pltpu.HBM)
    dma = pltpu.SemaphoreType.DMA
    shape = jax.ShapeDtypeStruct(coords.shape, F32)
    rows = lambda count, kind=F32: pltpu.VMEM((count, LANES), kind)
    field = pltpu.VMEM(coords.shape, F32)
    edges = pltpu.VMEM((times, 4, 3 * HROW, LANES), F32)
    messages = pltpu.VMEM((times, DEVS, 1, LANES), F32)
    return pl.pallas_call(
        body,
        out_shape=(shape, shape),
        in_specs=[apart] * 13,
        out_specs=(vmem, vmem),
        scratch_shapes=[
            field,
            field,
            field,
            field,
            pltpu.VMEM(elem_nodes.shape, I32),
            pltpu.VMEM(halo_lists.shape, I32),
            rows(NROW),
            rows(EROW),
            rows(CROW, I32),
            rows(CROW, I32),
            pltpu.VMEM(stiffness.shape, F32),
            pltpu.SMEM(block_class.shape, I32),
            pltpu.SMEM(tile_pairs.shape, I32),
            rows(3 * NROW),
            rows(3 * NROW),
            rows(3 * NROW),
            rows(3 * NROW),
            rows(EROW, I32),
            rows(12 * 16),
            rows(IDXROW, I32),
            rows(IDXROW, I32),
            rows(12 * EROW),
            rows(12 * EROW),
            rows(12 * EROW),
            rows(24 * EROW),
            rows(3 * NROW),
            rows(3 * NROW),
            rows(12 * HROW),
            rows(12 * HROW),
            pltpu.VMEM(((IDXROW + SROW) // 2, LANES, 2 * LANES), BF16),
            rows(2 * DEVS),
            rows(SROW, I32),
            rows(SROW, I32),
            rows(3 * SROW),
            rows(3 * SROW),
            rows(DEVS),
            edges,
            edges,
            edges,
            edges,
            messages,
            messages,
            dma((13,)),
            dma((times, 4)),
            dma((times, 4)),
            dma((times, 4)),
            dma((times, 4)),
            dma((times,)),
            dma((times,)),
        ],
        compiler_params=pltpu.CompilerParams(
            collective_id=0, has_side_effects=True, vmem_limit_bytes=60 * 1024 * 1024
        ),
    )(
        coords,
        displacement,
        velocity,
        ext_force,
        elem_nodes,
        halo_lists,
        inv_mass.reshape(NROW, LANES),
        thickness.reshape(EROW, LANES),
        contact_nodes.reshape(CROW, LANES),
        contact_bucket.reshape(CROW, LANES),
        stiffness,
        block_class,
        tile_pairs,
    )


def solution(mesh):
    split = P(None, ("px", "py"))
    line = P(("px", "py"))
    placed = (
        split,
        split,
        split,
        line,
        split,
        line,
        P(),
        split,
        line,
        split,
        line,
        P(("px", "py"), None),
        split,
    )
    return jax.shard_map(
        device_step,
        mesh=mesh,
        in_specs=placed,
        out_specs=(split, split),
        check_vma=False,
    )
```

```python
import jax
import jax.numpy as jnp
from jax import lax
from jax.experimental import pallas as pl
from jax.experimental.pallas import tpu as pltpu
from jax.sharding import PartitionSpec as P

MESH = pl.DeviceIdType.MESH
LANES = 128
EBLK = 128
STEPS = 2
SUBS = 2
FAR = 10000.0
DT = 0.05
PENALTY = 0.5
REACH = 4.0

N_PX = 16
N_PY = 8
DEVS = N_PX * N_PY
NROW = 16
EROW = 16
HROW = 4
XROW = NROW + 4 * HROW
CROW = 16
SROW = 32
CAP = 32
PAIRS = 16
IDXROW = 4 * EROW + 4 * HROW
UNROLL = 16
PAIR_UNROLL = 8

F32 = jnp.float32
BF16 = jnp.bfloat16
I32 = jnp.int32


def iota(shape, dim):
    return lax.broadcasted_iota(I32, shape, dim)


def halves(value):
    upper = value.astype(BF16).astype(F32)
    return upper, value - upper


def gather(tables, place, rows, high, first, onehot, number, found, target, add):
    unroll = min(UNROLL, rows // 2)
    numbers = iota((NROW, LANES), 0) + place

    def some(step, carry):
        for inner in range(unroll):
            tile = step * unroll + inner
            both = jnp.dot(
                tables, onehot[number + tile], preferred_element_type=F32
            )
            for side in range(2):
                row = tile * 2 + side
                here = jnp.broadcast_to(high[pl.ds(first + row, 1), :], (NROW, LANES)) == numbers
                lane = slice(side * LANES, (side + 1) * LANES)
                for c in range(3):
                    upper = both[c * NROW : (c + 1) * NROW, lane]
                    part = upper + both[(c + 3) * NROW : (c + 4) * NROW, lane]
                    total = jnp.sum(jnp.where(here, part, 0.0), axis=0, keepdims=True)
                    spot = pl.ds(target + c * rows + row, 1)
                    found[spot, :] = found[spot, :] + total if add else total
        return carry

    lax.fori_loop(0, rows // (2 * unroll), some, 0)


def split_table(table):
    return jnp.concatenate(halves(table), axis=0).astype(BF16)


def halve(values, halved, rows):
    upper, lower = halves(values[pl.ds(0, 3 * rows), :])
    halved[pl.ds(0, 3 * rows), :] = upper
    halved[pl.ds(3 * rows, 3 * rows), :] = lower


def scatter(halved, rows, high, first, onehot, number, place):
    unroll = min(UNROLL, rows // 2)
    numbers = (iota((NROW, LANES), 0) + place).astype(F32).astype(BF16)

    def some(step, total):
        columns, right = [], []
        for inner in range(2 * unroll):
            row = step * 2 * unroll + inner
            mine = jnp.broadcast_to(high[pl.ds(first + row, 1), :], (NROW, LANES))
            here = mine.astype(F32).astype(BF16) == numbers
            parts = []
            for part in range(6):
                value = jnp.broadcast_to(
                    halved[pl.ds(part * rows + row, 1), :], (NROW, LANES)
                ).astype(BF16)
                parts.append(jnp.where(here, value, jnp.zeros_like(value)))
            columns.append(jnp.concatenate(parts, axis=0))
        for inner in range(unroll):
            right.append(onehot[number + step * unroll + inner])
        return total + lax.dot_general(
            jnp.concatenate(columns, axis=1),
            jnp.concatenate(right, axis=1),
            (((1,), (1,)), ((), ())),
            preferred_element_type=F32,
        )

    total = lax.fori_loop(
        0, rows // (2 * unroll), some, jnp.zeros((6 * NROW, LANES), F32)
    )
    return total[: 3 * NROW] + total[3 * NROW :]


def build_onehots(low, first, rows, onehot, number):
    unroll = min(UNROLL, rows // 2)
    numbers = iota((LANES, LANES), 0)

    def some(step, carry):
        for inner in range(unroll):
            tile = step * unroll + inner
            for side in range(2):
                mine = low[pl.ds(first + tile * 2 + side, 1), :]
                here = jnp.broadcast_to(mine, (LANES, LANES)) == numbers
                ones = jnp.where(here, 1.0, 0.0).astype(BF16)
                onehot[number + tile, :, pl.ds(side * LANES, LANES)] = ones
        return carry

    lax.fori_loop(0, rows // (2 * unroll), some, 0)


def body(
    coords_hbm,
    displacement_hbm,
    velocity_hbm,
    ext_force_hbm,
    elem_nodes_hbm,
    halo_lists_hbm,
    inv_mass_hbm,
    thickness_hbm,
    contact_nodes_hbm,
    bucket_hbm,
    stiffness_hbm,
    block_class_hbm,
    tile_pairs_hbm,
    disp_out,
    vel_out,
    accel_out,
    coords,
    displacement,
    velocity,
    ext_force,
    elem_nodes,
    halo_lists,
    inv_mass,
    thickness,
    contact_nodes,
    bucket,
    stiffness,
    block_class,
    tile_pairs,
    base,
    disp,
    vel,
    fext,
    last,
    slow,
    spread,
    idx_low,
    idx_high,
    found,
    forces,
    held,
    halved,
    internal,
    contact,
    returned,
    ghosts,
    onehot,
    inverse,
    slot_low,
    slot_high,
    points,
    pushes,
    stage,
    halo_out,
    halo_in,
    back_out,
    back_in,
    slots_out,
    slots_in,
    loads,
    halo_sent,
    halo_got,
    back_sent,
    back_got,
    slots_sent,
    slots_got,
):
    sources = [
        bucket_hbm,
        contact_nodes_hbm,
        coords_hbm,
        displacement_hbm,
        halo_lists_hbm,
        elem_nodes_hbm,
        velocity_hbm,
        ext_force_hbm,
        inv_mass_hbm,
        thickness_hbm,
        stiffness_hbm,
        block_class_hbm,
        tile_pairs_hbm,
    ]
    targets = [
        bucket,
        contact_nodes,
        coords,
        displacement,
        halo_lists,
        elem_nodes,
        velocity,
        ext_force,
        inv_mass,
        thickness,
        stiffness,
        block_class,
        tile_pairs,
    ]
    copies = [
        pltpu.make_async_copy(source, target, loads.at[n])
        for n, (source, target) in enumerate(zip(sources, targets))
    ]
    for copy in copies:
        copy.start()

    i = lax.axis_index("px")
    j = lax.axis_index("py")
    me = i * N_PY + j
    neighbours = [
        (i > 0, (jnp.maximum(i - 1, 0), j)),
        (i < N_PX - 1, (jnp.minimum(i + 1, N_PX - 1), j)),
        (j > 0, (i, jnp.maximum(j - 1, 0))),
        (j < N_PY - 1, (i, jnp.minimum(j + 1, N_PY - 1))),
    ]
    facing = [1, 0, 3, 2]

    halo_in[...] = jnp.zeros_like(halo_in)
    back_in[...] = jnp.zeros_like(back_in)

    barrier = pltpu.get_barrier_semaphore()

    flips = [
        j + sum((1 - 2 * lax.rem(j // (1 << b), 2)) * (1 << b) for b in range(3) if mask >> b & 1)
        for mask in range(N_PY)
    ]

    def flip(mask):
        return sum(lax.rem(i // (1 << b) + mask // (1 << b), 2) * (1 << b) for b in range(4))

    def everyone(act):
        def some(step, carry):
            px = flip(N_PX - 1 - step)
            for py in flips[::-1]:
                act(px, py)
            return carry

        lax.fori_loop(0, N_PX - 1, some, 0)
        for py in flips[:0:-1]:
            act(i, py)

    def greet(px, py):
        pl.semaphore_signal(barrier, inc=1, device_id=(px, py), device_id_type=MESH)

    everyone(greet)

    def to_rows(source, target, count, rows):
        for c in range(count):
            for r in range(rows):
                target[pl.ds(c * rows + r, 1), :] = source[
                    pl.ds(c, 1), pl.ds(r * LANES, LANES)
                ]

    devs = iota((LANES, LANES), 0)
    lanes = iota((LANES, LANES), 1)
    earlier = jnp.concatenate(
        [jnp.where(devs < lanes, 1.0, 0.0), jnp.ones((LANES, LANES), F32)], axis=1
    ).astype(BF16)
    copies[0].wait()
    before = jnp.zeros((LANES, LANES), F32)
    named, ranks = [], []
    for row in range(CROW):
        here = jnp.broadcast_to(bucket[pl.ds(row, 1), :], (LANES, LANES)) == devs
        ones = jnp.where(here, 1.0, 0.0).astype(BF16)
        counts = jnp.dot(ones, earlier, preferred_element_type=F32)
        ranks.append(
            jnp.sum(jnp.where(here, counts[:, :LANES] + before, 0.0), axis=0, keepdims=True)
        )
        before = before + counts[:, LANES:]
        named.append(ones)

    copies[1].wait()
    slot_row = (devs & (CAP - 1)).astype(F32)
    nodes = jnp.zeros((LANES, 2 * LANES), F32)
    for row in range(0, CROW, 2):
        right = []
        for one in (row, row + 1):
            here = jnp.broadcast_to(ranks[one], (LANES, LANES)) == slot_row
            node = contact_nodes[pl.ds(one, 1), :]
            low = jnp.broadcast_to((node & (LANES - 1)).astype(F32), (LANES, LANES))
            high = jnp.broadcast_to(((node >> 7) + 1).astype(F32), (LANES, LANES))
            right.append(
                jnp.concatenate(
                    [jnp.where(here, low, 0.0), jnp.where(here, high, 0.0)], axis=0
                ).astype(BF16)
            )
        nodes = nodes + lax.dot_general(
            jnp.concatenate([named[row], named[row + 1]], axis=1),
            jnp.concatenate(right, axis=1),
            (((1,), (1,)), ((), ())),
            preferred_element_type=F32,
        )
    inverse[pl.ds(0, DEVS), :] = nodes[:, :LANES]
    inverse[pl.ds(DEVS, DEVS), :] = nodes[:, LANES:]
    block = iota((SROW, LANES), 1) >> 5
    low = jnp.zeros((SROW, LANES), F32)
    high = jnp.zeros((SROW, LANES), F32)
    for q in range(4):
        low = jnp.where(block == q, inverse[pl.ds(q, SROW, stride=4), :], low)
        high = jnp.where(block == q, inverse[pl.ds(DEVS + q, SROW, stride=4), :], high)
    slot_low[...] = low.astype(I32)
    slot_high[...] = high.astype(I32) - 1
    build_onehots(slot_low, 0, SROW, onehot, IDXROW // 2)

    copies[2].wait()
    copies[3].wait()
    to_rows(coords, base, 3, NROW)
    to_rows(displacement, disp, 3, NROW)

    def prepare_halo():
        copies[4].wait()
        for k in range(4):
            for r in range(HROW):
                entry = halo_lists[pl.ds(k, 1), pl.ds(r * LANES, LANES)]
                idx_low[pl.ds(4 * EROW + k * HROW + r, 1), :] = entry & (LANES - 1)
                idx_high[pl.ds(4 * EROW + k * HROW + r, 1), :] = entry >> 7
        build_onehots(idx_low, 4 * EROW, 4 * HROW, onehot, 2 * EROW)

    def prepare_rest():
        for copy in copies[5:]:
            copy.wait()
        for k in range(4):
            for r in range(EROW):
                entry = elem_nodes[pl.ds(k, 1), pl.ds(r * LANES, LANES)]
                idx_low[pl.ds(k * EROW + r, 1), :] = entry & (LANES - 1)
                idx_high[pl.ds(k * EROW + r, 1), :] = entry >> 7
        build_onehots(idx_low, 0, 4 * EROW, onehot, 0)
        to_rows(velocity, vel, 3, NROW)
        to_rows(ext_force, fext, 3, NROW)
        for r in range(EROW):
            slow[pl.ds(r, 1), :] = jnp.full((1, LANES), block_class[r], I32)
        for column in range(12):
            spread[pl.ds(column * 16, 12), :] = jnp.broadcast_to(
                stiffness[:, column : column + 1], (12, LANES)
            )

    def exchange_start(number, source, target, sent, got):
        for n, (exists, device) in enumerate(neighbours):

            @pl.when(exists)
            def _():
                pltpu.make_async_remote_copy(
                    src_ref=source.at[number, n],
                    dst_ref=target.at[number, facing[n]],
                    send_sem=sent.at[number, n],
                    recv_sem=got.at[number, facing[n]],
                    device_id=device,
                    device_id_type=MESH,
                ).start()

    def exchange_wait(number, buffer, sem):
        for n, (exists, _unused) in enumerate(neighbours):

            @pl.when(exists)
            def _():
                pltpu.make_async_copy(
                    buffer.at[number, n], buffer.at[number, n], sem.at[number, n]
                ).wait()

    def slots_start(number):
        def send(px, py):
            pltpu.make_async_remote_copy(
                src_ref=slots_out.at[number, px * N_PY + py],
                dst_ref=slots_in.at[number, me],
                send_sem=slots_sent.at[number],
                recv_sem=slots_got.at[number],
                device_id=(px, py),
                device_id_type=MESH,
            ).start()

        everyone(send)
        slots_in[number, me] = slots_out[number, me]

    def slots_wait(number, buffer, sem):
        part = buffer.at[number, pl.ds(0, DEVS - 1)]
        pltpu.make_async_copy(part, part, sem.at[number]).wait()

    def to_messages(parts, number):
        for q in range(4):
            mixed = jnp.zeros((SROW, LANES), F32)
            for c in range(3):
                shift = (CAP * (c - q)) % LANES
                turned = pltpu.roll(parts[c], shift, 1) if shift else parts[c]
                mixed = jnp.where(block == c, turned, mixed)
            stage[pl.ds(q * SROW, SROW), :] = mixed
        for a in range(SROW):
            for q in range(4):
                slots_out[number, 4 * a + q] = stage[pl.ds(q * SROW + a, 1), :]

    def from_messages(number):
        for a in range(SROW):
            for q in range(4):
                stage[pl.ds(q * SROW + a, 1), :] = slots_in[number, 4 * a + q]
        parts = []
        for c in range(3):
            mixed = jnp.zeros((SROW, LANES), F32)
            for q in range(4):
                shift = (CAP * (q - c)) % LANES
                rows = stage[pl.ds(q * SROW, SROW), :]
                turned = pltpu.roll(rows, shift, 1) if shift else rows
                mixed = jnp.where(block == q, turned, mixed)
            parts.append(mixed)
        return parts

    def send_points(number):
        gather(
            split_table(base[...] + disp[...]),
            0,
            SROW,
            slot_high,
            0,
            onehot,
            IDXROW // 2,
            points,
            0,
            False,
        )
        empty = slot_high[...] < 0
        to_messages(
            [jnp.where(empty, FAR, points[pl.ds(c * SROW, SROW), :]) for c in range(3)],
            number,
        )

    def push_tiles(number):
        for c, part in enumerate(from_messages(number)):
            points[pl.ds(c * SROW, SROW), :] = part
        numbers = iota((SROW, LANES), 0)

        def some_pairs(step, totals):
            for inner in range(PAIR_UNROLL):
                totals = one_pair(step * PAIR_UNROLL + inner, totals)
            return totals

        def one_pair(p, totals):
            first = tile_pairs[0, p]
            second = tile_pairs[1, p]
            mine = [
                jnp.broadcast_to(points[pl.ds(c * SROW + first, 1), :], (8, LANES))
                for c in range(3)
            ]
            others = [
                jnp.broadcast_to(points[pl.ds(c * SROW + second, 1), :], (8, LANES))
                for c in range(3)
            ]
            sums = [jnp.zeros((8, LANES), F32) for c in range(3)]
            for turn in range(LANES // 8):
                gap = [
                    mine[c] - pltpu.roll(others[c], turn * 8, 1, stride=1, stride_axis=0)
                    for c in range(3)
                ]
                dist = gap[0] * gap[0] + gap[1] * gap[1] + gap[2] * gap[2]
                weight = PENALTY * jnp.exp(dist * (-1.0 / REACH))
                sums = [sums[c] + weight * gap[c] for c in range(3)]
            return tuple(
                totals[c]
                + jnp.where(numbers == first, jnp.sum(sums[c], axis=0, keepdims=True), 0.0)
                for c in range(3)
            )

        zero = jnp.zeros((SROW, LANES), F32)
        return lax.fori_loop(0, PAIRS // PAIR_UNROLL, some_pairs, (zero, zero, zero))

    def list_edges(number):
        gather(
            split_table(disp[...]),
            0,
            4 * HROW,
            idx_high,
            4 * EROW,
            onehot,
            2 * EROW,
            returned,
            0,
            False,
        )
        for n in range(4):
            for c in range(3):
                halo_out[number, n, pl.ds(c * HROW, HROW), :] = returned[
                    pl.ds((c * 4 + n) * HROW, HROW), :
                ]

    def send_edges(number):
        exchange_start(number, halo_out, halo_in, halo_sent, halo_got)

    def own_corners():
        gather(
            split_table(disp[...]), 0, 4 * EROW, idx_high, 0, onehot, 0, found, 0, False
        )

    def element_stage(number, sub_no):
        exchange_wait(number, halo_in, halo_got)
        for n in range(4):
            for c in range(3):
                ghosts[pl.ds((c * 4 + n) * HROW, HROW), :] = halo_in[
                    number, n, pl.ds(c * HROW, HROW), :
                ]
        gather(
            split_table(ghosts[...]), NROW, 4 * EROW, idx_high, 0, onehot, 0, found, 0, True
        )
        local = [found[pl.ds(n * EROW, EROW), :] for n in range(12)]
        thick = thickness[...]
        for out in range(12):
            total = jnp.zeros((EROW, LANES), F32)
            for of in range(12):
                factor = spread[pl.ds(of * 16 + out, 1), :]
                total = total + jnp.broadcast_to(factor, (EROW, LANES)) * local[of]
            total = thick * total
            place = pl.ds(out * EROW, EROW)
            if sub_no == 0:
                held[place, :] = total
            else:
                total = jnp.where(slow[...] == 1, held[place, :], total)
            forces[place, :] = total
        halve(forces, halved, 4 * EROW)
        summed = scatter(halved, 4 * EROW, idx_high, 0, onehot, 0, NROW)
        for c in range(3):
            for n in range(4):
                first = (c * 4 + n) * HROW
                back_out[number, n, pl.ds(c * HROW, HROW), :] = summed[first : first + HROW]
        exchange_start(number, back_out, back_in, back_sent, back_got)

    def own_sums():
        internal[...] = scatter(halved, 4 * EROW, idx_high, 0, onehot, 0, 0)

    def return_stage(number):
        exchange_wait(number, back_in, back_got)
        for n in range(4):
            for c in range(3):
                returned[pl.ds(c * 4 * HROW + n * HROW, HROW), :] = back_in[
                    number, n, pl.ds(c * HROW, HROW), :
                ]
        halve(returned, halved, 4 * HROW)
        internal[...] = internal[...] + scatter(
            halved, 4 * HROW, idx_high, 4 * EROW, onehot, 2 * EROW, 0
        )

    def update():
        mass = inv_mass[...]
        for c in range(3):
            place = pl.ds(c * NROW, NROW)
            accel = mass * (fext[place, :] - internal[place, :] + contact[place, :])
            last[pl.ds(c * NROW, NROW), :] = disp[place, :]
            last[pl.ds((3 + c) * NROW, NROW), :] = vel[place, :]
            last[pl.ds((6 + c) * NROW, NROW), :] = accel
            speed = vel[place, :] + DT * accel
            vel[place, :] = speed
            disp[place, :] = disp[place, :] + DT * speed

    def major(step, carry):
        there, back = 2 * step, 2 * step + 1
        pl.when(step == 0)(prepare_halo)
        list_edges(there)
        send_points(there)

        @pl.when(step == 0)
        def _():
            pl.semaphore_wait(barrier, DEVS - 1)

        send_edges(there)
        slots_start(there)
        pl.when(step == 0)(prepare_rest)
        own_corners()
        element_stage(there, 0)
        slots_wait(there, slots_in, slots_got)
        to_messages(push_tiles(there), back)
        slots_start(back)
        own_sums()
        return_stage(there)
        slots_wait(back, slots_in, slots_got)
        for c, part in enumerate(from_messages(back)):
            pushes[pl.ds(c * SROW, SROW), :] = part
        halve(pushes, halved, SROW)
        contact[...] = scatter(halved, SROW, slot_high, 0, onehot, IDXROW // 2, 0)
        update()
        for sub_no in range(1, SUBS):
            list_edges(back)
            send_edges(back)
            own_corners()
            element_stage(back, sub_no)
            own_sums()
            return_stage(back)
            update()
        return carry

    lax.fori_loop(0, STEPS, major, 0)

    for c in range(3):
        for r in range(NROW):
            place = pl.ds(r * LANES, LANES)
            for n, out in enumerate((disp_out, vel_out, accel_out)):
                out[pl.ds(c, 1), place] = last[pl.ds((n * 3 + c) * NROW + r, 1), :]

    def drain(number, carry):
        exchange_wait(number, halo_out, halo_sent)
        exchange_wait(number, back_out, back_sent)
        slots_wait(number, slots_out, slots_sent)
        return carry

    lax.fori_loop(0, STEPS * SUBS, drain, 0)


def device_step(
    coords,
    displacement,
    velocity,
    inv_mass,
    ext_force,
    thickness,
    stiffness,
    elem_nodes,
    block_class,
    halo_lists,
    contact_nodes,
    contact_bucket,
    tile_pairs,
):
    times = STEPS * SUBS
    vmem = pl.BlockSpec(memory_space=pltpu.VMEM)
    apart = pl.BlockSpec(memory_space=pltpu.HBM)
    dma = pltpu.SemaphoreType.DMA
    shape = jax.ShapeDtypeStruct(coords.shape, F32)
    rows = lambda count, kind=F32: pltpu.VMEM((count, LANES), kind)
    field = pltpu.VMEM(coords.shape, F32)
    edges = pltpu.VMEM((times, 4, 3 * HROW, LANES), F32)
    messages = pltpu.VMEM((times, DEVS, 1, LANES), F32)
    disp, vel, accel = pl.pallas_call(
        body,
        out_shape=(shape, shape, shape),
        in_specs=[apart] * 13,
        out_specs=(vmem, vmem, vmem),
        scratch_shapes=[
            field,
            field,
            field,
            field,
            pltpu.VMEM(elem_nodes.shape, I32),
            pltpu.VMEM(halo_lists.shape, I32),
            rows(NROW),
            rows(EROW),
            rows(CROW, I32),
            rows(CROW, I32),
            pltpu.VMEM(stiffness.shape, F32),
            pltpu.SMEM(block_class.shape, I32),
            pltpu.SMEM(tile_pairs.shape, I32),
            rows(3 * NROW),
            rows(3 * NROW),
            rows(3 * NROW),
            rows(3 * NROW),
            rows(9 * NROW),
            rows(EROW, I32),
            rows(12 * 16),
            rows(IDXROW, I32),
            rows(IDXROW, I32),
            rows(12 * EROW),
            rows(12 * EROW),
            rows(12 * EROW),
            rows(24 * EROW),
            rows(3 * NROW),
            rows(3 * NROW),
            rows(12 * HROW),
            rows(12 * HROW),
            pltpu.VMEM(((IDXROW + SROW) // 2, LANES, 2 * LANES), BF16),
            rows(2 * DEVS),
            rows(SROW, I32),
            rows(SROW, I32),
            rows(3 * SROW),
            rows(3 * SROW),
            rows(DEVS),
            edges,
            edges,
            edges,
            edges,
            messages,
            messages,
            dma((13,)),
            dma((times, 4)),
            dma((times, 4)),
            dma((times, 4)),
            dma((times, 4)),
            dma((times,)),
            dma((times,)),
        ],
        compiler_params=pltpu.CompilerParams(
            collective_id=0, has_side_effects=True, vmem_limit_bytes=60 * 1024 * 1024
        ),
    )(
        coords,
        displacement,
        velocity,
        ext_force,
        elem_nodes,
        halo_lists,
        inv_mass.reshape(NROW, LANES),
        thickness.reshape(EROW, LANES),
        contact_nodes.reshape(CROW, LANES),
        contact_bucket.reshape(CROW, LANES),
        stiffness,
        block_class,
        tile_pairs,
    )
    vel = vel + DT * accel
    return disp + DT * vel, vel


def solution(mesh):
    split = P(None, ("px", "py"))
    line = P(("px", "py"))
    placed = (
        split,
        split,
        split,
        line,
        split,
        line,
        P(),
        split,
        line,
        split,
        line,
        P(("px", "py"), None),
        split,
    )
    return jax.shard_map(
        device_step,
        mesh=mesh,
        in_specs=placed,
        out_specs=(split, split),
        check_vma=False,
    )
```

```python
import jax
import jax.numpy as jnp
from jax import lax
from jax.experimental import pallas as pl
from jax.experimental.pallas import tpu as pltpu
from jax.sharding import PartitionSpec as P

MESH = pl.DeviceIdType.MESH
LANES = 128
EBLK = 128
STEPS = 2
SUBS = 2
FAR = 10000.0
DT = 0.05
PENALTY = 0.5
REACH = 4.0

N_PX = 16
N_PY = 8
DEVS = N_PX * N_PY
NROW = 16
EROW = 16
HROW = 4
XROW = NROW + 4 * HROW
CROW = 16
SROW = 32
CAP = 32
PAIRS = 16
IDXROW = 4 * EROW + 4 * HROW
UNROLL = 16
PAIR_UNROLL = 8

F32 = jnp.float32
BF16 = jnp.bfloat16
I32 = jnp.int32


def iota(shape, dim):
    return lax.broadcasted_iota(I32, shape, dim)


def halves(value):
    upper = value.astype(BF16).astype(F32)
    return upper, value - upper


def gather(tables, place, rows, high, first, onehot, number, found, target, add):
    unroll = min(UNROLL, rows // 2)
    numbers = iota((NROW, LANES), 0) + place

    def some(step, carry):
        for inner in range(unroll):
            tile = step * unroll + inner
            both = jnp.dot(
                tables, onehot[number + tile], preferred_element_type=F32
            )
            for side in range(2):
                row = tile * 2 + side
                here = jnp.broadcast_to(high[pl.ds(first + row, 1), :], (NROW, LANES)) == numbers
                lane = slice(side * LANES, (side + 1) * LANES)
                for c in range(3):
                    upper = both[c * NROW : (c + 1) * NROW, lane]
                    part = upper + both[(c + 3) * NROW : (c + 4) * NROW, lane]
                    total = jnp.sum(jnp.where(here, part, 0.0), axis=0, keepdims=True)
                    spot = pl.ds(target + c * rows + row, 1)
                    found[spot, :] = found[spot, :] + total if add else total
        return carry

    lax.fori_loop(0, rows // (2 * unroll), some, 0)


def split_table(table):
    return jnp.concatenate(halves(table), axis=0).astype(BF16)


def halve(values, halved, rows):
    upper, lower = halves(values[pl.ds(0, 3 * rows), :])
    halved[pl.ds(0, 3 * rows), :] = upper
    halved[pl.ds(3 * rows, 3 * rows), :] = lower


def scatter(halved, rows, high, first, onehot, number, place):
    unroll = min(UNROLL, rows // 2)
    numbers = (iota((NROW, LANES), 0) + place).astype(F32).astype(BF16)

    def some(step, total):
        columns, right = [], []
        for inner in range(2 * unroll):
            row = step * 2 * unroll + inner
            mine = jnp.broadcast_to(high[pl.ds(first + row, 1), :], (NROW, LANES))
            here = mine.astype(F32).astype(BF16) == numbers
            parts = []
            for part in range(6):
                value = jnp.broadcast_to(
                    halved[pl.ds(part * rows + row, 1), :], (NROW, LANES)
                ).astype(BF16)
                parts.append(jnp.where(here, value, jnp.zeros_like(value)))
            columns.append(jnp.concatenate(parts, axis=0))
        for inner in range(unroll):
            right.append(onehot[number + step * unroll + inner])
        return total + lax.dot_general(
            jnp.concatenate(columns, axis=1),
            jnp.concatenate(right, axis=1),
            (((1,), (1,)), ((), ())),
            preferred_element_type=F32,
        )

    total = lax.fori_loop(
        0, rows // (2 * unroll), some, jnp.zeros((6 * NROW, LANES), F32)
    )
    return total[: 3 * NROW] + total[3 * NROW :]


def build_onehots(low, first, rows, onehot, number):
    unroll = min(UNROLL, rows // 2)
    numbers = iota((LANES, LANES), 0)

    def some(step, carry):
        for inner in range(unroll):
            tile = step * unroll + inner
            for side in range(2):
                mine = low[pl.ds(first + tile * 2 + side, 1), :]
                here = jnp.broadcast_to(mine, (LANES, LANES)) == numbers
                ones = jnp.where(here, 1.0, 0.0).astype(BF16)
                onehot[number + tile, :, pl.ds(side * LANES, LANES)] = ones
        return carry

    lax.fori_loop(0, rows // (2 * unroll), some, 0)


def body(
    coords_hbm,
    displacement_hbm,
    velocity_hbm,
    ext_force_hbm,
    elem_nodes_hbm,
    halo_lists_hbm,
    inv_mass_hbm,
    thickness_hbm,
    contact_nodes_hbm,
    bucket_hbm,
    stiffness_hbm,
    block_class_hbm,
    tile_pairs_hbm,
    disp_out,
    vel_out,
    accel_out,
    coords,
    displacement,
    velocity,
    ext_force,
    elem_nodes,
    halo_lists,
    inv_mass,
    thickness,
    contact_nodes,
    bucket,
    stiffness,
    block_class,
    tile_pairs,
    base,
    disp,
    vel,
    fext,
    last,
    slow,
    spread,
    idx_low,
    idx_high,
    found,
    forces,
    held,
    halved,
    internal,
    contact,
    returned,
    ghosts,
    onehot,
    inverse,
    slot_low,
    slot_high,
    points,
    pushes,
    stage,
    halo_out,
    halo_in,
    back_out,
    back_in,
    slots_out,
    slots_in,
    loads,
    halo_sent,
    halo_got,
    back_sent,
    back_got,
    slots_sent,
    slots_got,
):
    sources = [
        bucket_hbm,
        contact_nodes_hbm,
        coords_hbm,
        displacement_hbm,
        halo_lists_hbm,
        elem_nodes_hbm,
        velocity_hbm,
        ext_force_hbm,
        inv_mass_hbm,
        thickness_hbm,
        stiffness_hbm,
        block_class_hbm,
        tile_pairs_hbm,
    ]
    targets = [
        bucket,
        contact_nodes,
        coords,
        displacement,
        halo_lists,
        elem_nodes,
        velocity,
        ext_force,
        inv_mass,
        thickness,
        stiffness,
        block_class,
        tile_pairs,
    ]
    copies = [
        pltpu.make_async_copy(source, target, loads.at[n])
        for n, (source, target) in enumerate(zip(sources, targets))
    ]
    for copy in copies:
        copy.start()

    i = lax.axis_index("px")
    j = lax.axis_index("py")
    me = i * N_PY + j
    neighbours = [
        (i > 0, (jnp.maximum(i - 1, 0), j)),
        (i < N_PX - 1, (jnp.minimum(i + 1, N_PX - 1), j)),
        (j > 0, (i, jnp.maximum(j - 1, 0))),
        (j < N_PY - 1, (i, jnp.minimum(j + 1, N_PY - 1))),
    ]
    facing = [1, 0, 3, 2]

    halo_in[...] = jnp.zeros_like(halo_in)
    back_in[...] = jnp.zeros_like(back_in)

    barrier = pltpu.get_barrier_semaphore()

    flips = [
        j + sum((1 - 2 * lax.rem(j // (1 << b), 2)) * (1 << b) for b in range(3) if mask >> b & 1)
        for mask in range(N_PY)
    ]

    def flip(mask):
        return sum(lax.rem(i // (1 << b) + mask // (1 << b), 2) * (1 << b) for b in range(4))

    def everyone(act):
        for mask in range(N_PX - 1, 0, -1):
            px = flip(mask)
            for py in flips[::-1]:
                act(px, py)
        for py in flips[:0:-1]:
            act(i, py)

    def greet(px, py):
        pl.semaphore_signal(barrier, inc=1, device_id=(px, py), device_id_type=MESH)

    everyone(greet)

    def to_rows(source, target, count, rows):
        for c in range(count):
            for r in range(rows):
                target[pl.ds(c * rows + r, 1), :] = source[
                    pl.ds(c, 1), pl.ds(r * LANES, LANES)
                ]

    devs = iota((LANES, LANES), 0)
    lanes = iota((LANES, LANES), 1)
    earlier = jnp.concatenate(
        [jnp.where(devs < lanes, 1.0, 0.0), jnp.ones((LANES, LANES), F32)], axis=1
    ).astype(BF16)
    copies[0].wait()
    before = jnp.zeros((LANES, LANES), F32)
    named, ranks = [], []
    for row in range(CROW):
        here = jnp.broadcast_to(bucket[pl.ds(row, 1), :], (LANES, LANES)) == devs
        ones = jnp.where(here, 1.0, 0.0).astype(BF16)
        counts = jnp.dot(ones, earlier, preferred_element_type=F32)
        ranks.append(
            jnp.sum(jnp.where(here, counts[:, :LANES] + before, 0.0), axis=0, keepdims=True)
        )
        before = before + counts[:, LANES:]
        named.append(ones)

    copies[1].wait()
    slot_row = (devs & (CAP - 1)).astype(F32)
    nodes = jnp.zeros((LANES, 2 * LANES), F32)
    for row in range(0, CROW, 2):
        right = []
        for one in (row, row + 1):
            here = jnp.broadcast_to(ranks[one], (LANES, LANES)) == slot_row
            node = contact_nodes[pl.ds(one, 1), :]
            low = jnp.broadcast_to((node & (LANES - 1)).astype(F32), (LANES, LANES))
            high = jnp.broadcast_to(((node >> 7) + 1).astype(F32), (LANES, LANES))
            right.append(
                jnp.concatenate(
                    [jnp.where(here, low, 0.0), jnp.where(here, high, 0.0)], axis=0
                ).astype(BF16)
            )
        nodes = nodes + lax.dot_general(
            jnp.concatenate([named[row], named[row + 1]], axis=1),
            jnp.concatenate(right, axis=1),
            (((1,), (1,)), ((), ())),
            preferred_element_type=F32,
        )
    inverse[pl.ds(0, DEVS), :] = nodes[:, :LANES]
    inverse[pl.ds(DEVS, DEVS), :] = nodes[:, LANES:]
    block = iota((SROW, LANES), 1) >> 5
    low = jnp.zeros((SROW, LANES), F32)
    high = jnp.zeros((SROW, LANES), F32)
    for q in range(4):
        low = jnp.where(block == q, inverse[pl.ds(q, SROW, stride=4), :], low)
        high = jnp.where(block == q, inverse[pl.ds(DEVS + q, SROW, stride=4), :], high)
    slot_low[...] = low.astype(I32)
    slot_high[...] = high.astype(I32) - 1
    build_onehots(slot_low, 0, SROW, onehot, IDXROW // 2)

    copies[2].wait()
    copies[3].wait()
    to_rows(coords, base, 3, NROW)
    to_rows(displacement, disp, 3, NROW)

    def prepare_halo():
        copies[4].wait()
        for k in range(4):
            for r in range(HROW):
                entry = halo_lists[pl.ds(k, 1), pl.ds(r * LANES, LANES)]
                idx_low[pl.ds(4 * EROW + k * HROW + r, 1), :] = entry & (LANES - 1)
                idx_high[pl.ds(4 * EROW + k * HROW + r, 1), :] = entry >> 7
        build_onehots(idx_low, 4 * EROW, 4 * HROW, onehot, 2 * EROW)

    def prepare_rest():
        for copy in copies[5:]:
            copy.wait()
        for k in range(4):
            for r in range(EROW):
                entry = elem_nodes[pl.ds(k, 1), pl.ds(r * LANES, LANES)]
                idx_low[pl.ds(k * EROW + r, 1), :] = entry & (LANES - 1)
                idx_high[pl.ds(k * EROW + r, 1), :] = entry >> 7
        build_onehots(idx_low, 0, 4 * EROW, onehot, 0)
        to_rows(velocity, vel, 3, NROW)
        to_rows(ext_force, fext, 3, NROW)
        for r in range(EROW):
            slow[pl.ds(r, 1), :] = jnp.full((1, LANES), block_class[r], I32)
        for column in range(12):
            spread[pl.ds(column * 16, 12), :] = jnp.broadcast_to(
                stiffness[:, column : column + 1], (12, LANES)
            )

    def exchange_start(number, source, target, sent, got):
        for n, (exists, device) in enumerate(neighbours):

            @pl.when(exists)
            def _():
                pltpu.make_async_remote_copy(
                    src_ref=source.at[number, n],
                    dst_ref=target.at[number, facing[n]],
                    send_sem=sent.at[number, n],
                    recv_sem=got.at[number, facing[n]],
                    device_id=device,
                    device_id_type=MESH,
                ).start()

    def exchange_wait(number, buffer, sem):
        for n, (exists, _unused) in enumerate(neighbours):

            @pl.when(exists)
            def _():
                pltpu.make_async_copy(
                    buffer.at[number, n], buffer.at[number, n], sem.at[number, n]
                ).wait()

    def slots_start(number):
        def send(px, py):
            pltpu.make_async_remote_copy(
                src_ref=slots_out.at[number, px * N_PY + py],
                dst_ref=slots_in.at[number, me],
                send_sem=slots_sent.at[number],
                recv_sem=slots_got.at[number],
                device_id=(px, py),
                device_id_type=MESH,
            ).start()

        everyone(send)
        slots_in[number, me] = slots_out[number, me]

    def slots_wait(number, buffer, sem):
        part = buffer.at[number, pl.ds(0, DEVS - 1)]
        pltpu.make_async_copy(part, part, sem.at[number]).wait()

    def to_messages(parts, number):
        for q in range(4):
            mixed = jnp.zeros((SROW, LANES), F32)
            for c in range(3):
                shift = (CAP * (c - q)) % LANES
                turned = pltpu.roll(parts[c], shift, 1) if shift else parts[c]
                mixed = jnp.where(block == c, turned, mixed)
            stage[pl.ds(q * SROW, SROW), :] = mixed
        for a in range(SROW):
            for q in range(4):
                slots_out[number, 4 * a + q] = stage[pl.ds(q * SROW + a, 1), :]

    def from_messages(number):
        for a in range(SROW):
            for q in range(4):
                stage[pl.ds(q * SROW + a, 1), :] = slots_in[number, 4 * a + q]
        parts = []
        for c in range(3):
            mixed = jnp.zeros((SROW, LANES), F32)
            for q in range(4):
                shift = (CAP * (q - c)) % LANES
                rows = stage[pl.ds(q * SROW, SROW), :]
                turned = pltpu.roll(rows, shift, 1) if shift else rows
                mixed = jnp.where(block == q, turned, mixed)
            parts.append(mixed)
        return parts

    def send_points(number):
        gather(
            split_table(base[...] + disp[...]),
            0,
            SROW,
            slot_high,
            0,
            onehot,
            IDXROW // 2,
            points,
            0,
            False,
        )
        empty = slot_high[...] < 0
        to_messages(
            [jnp.where(empty, FAR, points[pl.ds(c * SROW, SROW), :]) for c in range(3)],
            number,
        )

    def push_tiles(number):
        for c, part in enumerate(from_messages(number)):
            points[pl.ds(c * SROW, SROW), :] = part
        numbers = iota((SROW, LANES), 0)

        def some_pairs(step, totals):
            for inner in range(PAIR_UNROLL):
                totals = one_pair(step * PAIR_UNROLL + inner, totals)
            return totals

        def one_pair(p, totals):
            first = tile_pairs[0, p]
            second = tile_pairs[1, p]
            mine = [
                jnp.broadcast_to(points[pl.ds(c * SROW + first, 1), :], (8, LANES))
                for c in range(3)
            ]
            others = [
                jnp.broadcast_to(points[pl.ds(c * SROW + second, 1), :], (8, LANES))
                for c in range(3)
            ]
            sums = [jnp.zeros((8, LANES), F32) for c in range(3)]
            for turn in range(LANES // 8):
                gap = [
                    mine[c] - pltpu.roll(others[c], turn * 8, 1, stride=1, stride_axis=0)
                    for c in range(3)
                ]
                dist = gap[0] * gap[0] + gap[1] * gap[1] + gap[2] * gap[2]
                weight = PENALTY * jnp.exp(dist * (-1.0 / REACH))
                sums = [sums[c] + weight * gap[c] for c in range(3)]
            return tuple(
                totals[c]
                + jnp.where(numbers == first, jnp.sum(sums[c], axis=0, keepdims=True), 0.0)
                for c in range(3)
            )

        zero = jnp.zeros((SROW, LANES), F32)
        return lax.fori_loop(0, PAIRS // PAIR_UNROLL, some_pairs, (zero, zero, zero))

    def list_edges(number):
        gather(
            split_table(disp[...]),
            0,
            4 * HROW,
            idx_high,
            4 * EROW,
            onehot,
            2 * EROW,
            returned,
            0,
            False,
        )
        for n in range(4):
            for c in range(3):
                halo_out[number, n, pl.ds(c * HROW, HROW), :] = returned[
                    pl.ds((c * 4 + n) * HROW, HROW), :
                ]

    def send_edges(number):
        exchange_start(number, halo_out, halo_in, halo_sent, halo_got)

    def own_corners():
        gather(
            split_table(disp[...]), 0, 4 * EROW, idx_high, 0, onehot, 0, found, 0, False
        )

    def element_stage(number, sub_no):
        exchange_wait(number, halo_in, halo_got)
        for n in range(4):
            for c in range(3):
                ghosts[pl.ds((c * 4 + n) * HROW, HROW), :] = halo_in[
                    number, n, pl.ds(c * HROW, HROW), :
                ]
        gather(
            split_table(ghosts[...]), NROW, 4 * EROW, idx_high, 0, onehot, 0, found, 0, True
        )
        local = [found[pl.ds(n * EROW, EROW), :] for n in range(12)]
        thick = thickness[...]
        for out in range(12):
            total = jnp.zeros((EROW, LANES), F32)
            for of in range(12):
                factor = spread[pl.ds(of * 16 + out, 1), :]
                total = total + jnp.broadcast_to(factor, (EROW, LANES)) * local[of]
            total = thick * total
            place = pl.ds(out * EROW, EROW)
            if sub_no == 0:
                held[place, :] = total
            else:
                total = jnp.where(slow[...] == 1, held[place, :], total)
            forces[place, :] = total
        halve(forces, halved, 4 * EROW)
        summed = scatter(halved, 4 * EROW, idx_high, 0, onehot, 0, NROW)
        for c in range(3):
            for n in range(4):
                first = (c * 4 + n) * HROW
                back_out[number, n, pl.ds(c * HROW, HROW), :] = summed[first : first + HROW]
        exchange_start(number, back_out, back_in, back_sent, back_got)

    def own_sums():
        internal[...] = scatter(halved, 4 * EROW, idx_high, 0, onehot, 0, 0)

    def return_stage(number):
        exchange_wait(number, back_in, back_got)
        for n in range(4):
            for c in range(3):
                returned[pl.ds(c * 4 * HROW + n * HROW, HROW), :] = back_in[
                    number, n, pl.ds(c * HROW, HROW), :
                ]
        halve(returned, halved, 4 * HROW)
        internal[...] = internal[...] + scatter(
            halved, 4 * HROW, idx_high, 4 * EROW, onehot, 2 * EROW, 0
        )

    def update():
        mass = inv_mass[...]
        for c in range(3):
            place = pl.ds(c * NROW, NROW)
            accel = mass * (fext[place, :] - internal[place, :] + contact[place, :])
            last[pl.ds(c * NROW, NROW), :] = disp[place, :]
            last[pl.ds((3 + c) * NROW, NROW), :] = vel[place, :]
            last[pl.ds((6 + c) * NROW, NROW), :] = accel
            speed = vel[place, :] + DT * accel
            vel[place, :] = speed
            disp[place, :] = disp[place, :] + DT * speed

    def major(step, carry):
        there, back = 2 * step, 2 * step + 1
        pl.when(step == 0)(prepare_halo)
        list_edges(there)
        send_points(there)

        @pl.when(step == 0)
        def _():
            pl.semaphore_wait(barrier, DEVS - 1)

        send_edges(there)
        slots_start(there)
        pl.when(step == 0)(prepare_rest)
        own_corners()
        element_stage(there, 0)
        slots_wait(there, slots_in, slots_got)
        to_messages(push_tiles(there), back)
        slots_start(back)
        own_sums()
        return_stage(there)
        slots_wait(back, slots_in, slots_got)
        for c, part in enumerate(from_messages(back)):
            pushes[pl.ds(c * SROW, SROW), :] = part
        halve(pushes, halved, SROW)
        contact[...] = scatter(halved, SROW, slot_high, 0, onehot, IDXROW // 2, 0)
        update()
        for sub_no in range(1, SUBS):
            list_edges(back)
            send_edges(back)
            own_corners()
            element_stage(back, sub_no)
            own_sums()
            return_stage(back)
            update()
        return carry

    lax.fori_loop(0, STEPS, major, 0)

    for c in range(3):
        for r in range(NROW):
            place = pl.ds(r * LANES, LANES)
            for n, out in enumerate((disp_out, vel_out, accel_out)):
                out[pl.ds(c, 1), place] = last[pl.ds((n * 3 + c) * NROW + r, 1), :]

    def drain(number, carry):
        exchange_wait(number, halo_out, halo_sent)
        exchange_wait(number, back_out, back_sent)
        slots_wait(number, slots_out, slots_sent)
        return carry

    lax.fori_loop(0, STEPS * SUBS, drain, 0)


def device_step(
    coords,
    displacement,
    velocity,
    inv_mass,
    ext_force,
    thickness,
    stiffness,
    elem_nodes,
    block_class,
    halo_lists,
    contact_nodes,
    contact_bucket,
    tile_pairs,
):
    times = STEPS * SUBS
    vmem = pl.BlockSpec(memory_space=pltpu.VMEM)
    apart = pl.BlockSpec(memory_space=pltpu.HBM)
    dma = pltpu.SemaphoreType.DMA
    shape = jax.ShapeDtypeStruct(coords.shape, F32)
    rows = lambda count, kind=F32: pltpu.VMEM((count, LANES), kind)
    field = pltpu.VMEM(coords.shape, F32)
    edges = pltpu.VMEM((times, 4, 3 * HROW, LANES), F32)
    messages = pltpu.VMEM((times, DEVS, 1, LANES), F32)
    disp, vel, accel = pl.pallas_call(
        body,
        out_shape=(shape, shape, shape),
        in_specs=[apart] * 13,
        out_specs=(vmem, vmem, vmem),
        scratch_shapes=[
            field,
            field,
            field,
            field,
            pltpu.VMEM(elem_nodes.shape, I32),
            pltpu.VMEM(halo_lists.shape, I32),
            rows(NROW),
            rows(EROW),
            rows(CROW, I32),
            rows(CROW, I32),
            pltpu.VMEM(stiffness.shape, F32),
            pltpu.SMEM(block_class.shape, I32),
            pltpu.SMEM(tile_pairs.shape, I32),
            rows(3 * NROW),
            rows(3 * NROW),
            rows(3 * NROW),
            rows(3 * NROW),
            rows(9 * NROW),
            rows(EROW, I32),
            rows(12 * 16),
            rows(IDXROW, I32),
            rows(IDXROW, I32),
            rows(12 * EROW),
            rows(12 * EROW),
            rows(12 * EROW),
            rows(24 * EROW),
            rows(3 * NROW),
            rows(3 * NROW),
            rows(12 * HROW),
            rows(12 * HROW),
            pltpu.VMEM(((IDXROW + SROW) // 2, LANES, 2 * LANES), BF16),
            rows(2 * DEVS),
            rows(SROW, I32),
            rows(SROW, I32),
            rows(3 * SROW),
            rows(3 * SROW),
            rows(DEVS),
            edges,
            edges,
            edges,
            edges,
            messages,
            messages,
            dma((13,)),
            dma((times, 4)),
            dma((times, 4)),
            dma((times, 4)),
            dma((times, 4)),
            dma((times,)),
            dma((times,)),
        ],
        compiler_params=pltpu.CompilerParams(
            collective_id=0, has_side_effects=True, vmem_limit_bytes=60 * 1024 * 1024
        ),
    )(
        coords,
        displacement,
        velocity,
        ext_force,
        elem_nodes,
        halo_lists,
        inv_mass.reshape(NROW, LANES),
        thickness.reshape(EROW, LANES),
        contact_nodes.reshape(CROW, LANES),
        contact_bucket.reshape(CROW, LANES),
        stiffness,
        block_class,
        tile_pairs,
    )
    vel = vel + DT * accel
    return disp + DT * vel, vel


def solution(mesh):
    split = P(None, ("px", "py"))
    line = P(("px", "py"))
    placed = (
        split,
        split,
        split,
        line,
        split,
        line,
        P(),
        split,
        line,
        split,
        line,
        P(("px", "py"), None),
        split,
    )
    return jax.shard_map(
        device_step,
        mesh=mesh,
        in_specs=placed,
        out_specs=(split, split),
        check_vma=False,
    )
```

```python
import jax
import jax.numpy as jnp
from jax import lax
from jax.experimental import pallas as pl
from jax.experimental.pallas import tpu as pltpu
from jax.sharding import PartitionSpec as P

MESH = pl.DeviceIdType.MESH
LANES = 128
EBLK = 128
STEPS = 2
SUBS = 2
FAR = 10000.0
DT = 0.05
PENALTY = 0.5
REACH = 4.0

N_PX = 16
N_PY = 8
DEVS = N_PX * N_PY
NROW = 16
EROW = 16
HROW = 4
XROW = NROW + 4 * HROW
CROW = 16
SROW = 32
CAP = 32
PAIRS = 16
IDXROW = 4 * EROW + 4 * HROW
UNROLL = 16
PAIR_UNROLL = 8

F32 = jnp.float32
BF16 = jnp.bfloat16
I32 = jnp.int32


def iota(shape, dim):
    return lax.broadcasted_iota(I32, shape, dim)


def halves(value):
    upper = value.astype(BF16).astype(F32)
    return upper, value - upper


def gather(tables, place, rows, high, first, onehot, number, found, target, add):
    unroll = min(UNROLL, rows // 2)
    numbers = iota((NROW, LANES), 0) + place

    def some(step, carry):
        for inner in range(unroll):
            tile = step * unroll + inner
            both = jnp.dot(
                tables, onehot[number + tile], preferred_element_type=F32
            )
            for side in range(2):
                row = tile * 2 + side
                here = jnp.broadcast_to(high[pl.ds(first + row, 1), :], (NROW, LANES)) == numbers
                lane = slice(side * LANES, (side + 1) * LANES)
                for c in range(3):
                    upper = both[c * NROW : (c + 1) * NROW, lane]
                    part = upper + both[(c + 3) * NROW : (c + 4) * NROW, lane]
                    total = jnp.sum(jnp.where(here, part, 0.0), axis=0, keepdims=True)
                    spot = pl.ds(target + c * rows + row, 1)
                    found[spot, :] = found[spot, :] + total if add else total
        return carry

    lax.fori_loop(0, rows // (2 * unroll), some, 0)


def split_table(table):
    return jnp.concatenate(halves(table), axis=0).astype(BF16)


def halve(values, halved, rows):
    upper, lower = halves(values[pl.ds(0, 3 * rows), :])
    halved[pl.ds(0, 3 * rows), :] = upper
    halved[pl.ds(3 * rows, 3 * rows), :] = lower


def scatter(halved, rows, high, first, onehot, number, place):
    unroll = min(UNROLL, rows // 2)
    numbers = (iota((NROW, LANES), 0) + place).astype(F32).astype(BF16)

    def some(step, total):
        columns, right = [], []
        for inner in range(2 * unroll):
            row = step * 2 * unroll + inner
            mine = jnp.broadcast_to(high[pl.ds(first + row, 1), :], (NROW, LANES))
            here = mine.astype(F32).astype(BF16) == numbers
            parts = []
            for part in range(6):
                value = jnp.broadcast_to(
                    halved[pl.ds(part * rows + row, 1), :], (NROW, LANES)
                ).astype(BF16)
                parts.append(jnp.where(here, value, jnp.zeros_like(value)))
            columns.append(jnp.concatenate(parts, axis=0))
        for inner in range(unroll):
            right.append(onehot[number + step * unroll + inner])
        return total + lax.dot_general(
            jnp.concatenate(columns, axis=1),
            jnp.concatenate(right, axis=1),
            (((1,), (1,)), ((), ())),
            preferred_element_type=F32,
        )

    total = lax.fori_loop(
        0, rows // (2 * unroll), some, jnp.zeros((6 * NROW, LANES), F32)
    )
    return total[: 3 * NROW] + total[3 * NROW :]


def build_onehots(low, first, rows, onehot, number):
    unroll = min(UNROLL, rows // 2)
    numbers = iota((LANES, LANES), 0)

    def some(step, carry):
        for inner in range(unroll):
            tile = step * unroll + inner
            for side in range(2):
                mine = low[pl.ds(first + tile * 2 + side, 1), :]
                here = jnp.broadcast_to(mine, (LANES, LANES)) == numbers
                ones = jnp.where(here, 1.0, 0.0).astype(BF16)
                onehot[number + tile, :, pl.ds(side * LANES, LANES)] = ones
        return carry

    lax.fori_loop(0, rows // (2 * unroll), some, 0)


def body(
    coords_hbm,
    displacement_hbm,
    velocity_hbm,
    ext_force_hbm,
    elem_nodes_hbm,
    halo_lists_hbm,
    inv_mass_hbm,
    thickness_hbm,
    contact_nodes_hbm,
    bucket_hbm,
    stiffness_hbm,
    block_class_hbm,
    tile_pairs_hbm,
    disp_out,
    vel_out,
    accel_out,
    coords,
    displacement,
    velocity,
    ext_force,
    elem_nodes,
    halo_lists,
    inv_mass,
    thickness,
    contact_nodes,
    bucket,
    stiffness,
    block_class,
    tile_pairs,
    base,
    disp,
    vel,
    fext,
    last,
    slow,
    spread,
    idx_low,
    idx_high,
    found,
    forces,
    held,
    halved,
    internal,
    contact,
    returned,
    ghosts,
    onehot,
    inverse,
    slot_low,
    slot_high,
    points,
    pushes,
    stage,
    halo_out,
    halo_in,
    back_out,
    back_in,
    slots_out,
    slots_in,
    loads,
    halo_sent,
    halo_got,
    back_sent,
    back_got,
    slots_sent,
    slots_got,
):
    sources = [
        bucket_hbm,
        contact_nodes_hbm,
        coords_hbm,
        displacement_hbm,
        halo_lists_hbm,
        elem_nodes_hbm,
        velocity_hbm,
        ext_force_hbm,
        inv_mass_hbm,
        thickness_hbm,
        stiffness_hbm,
        block_class_hbm,
        tile_pairs_hbm,
    ]
    targets = [
        bucket,
        contact_nodes,
        coords,
        displacement,
        halo_lists,
        elem_nodes,
        velocity,
        ext_force,
        inv_mass,
        thickness,
        stiffness,
        block_class,
        tile_pairs,
    ]
    copies = [
        pltpu.make_async_copy(source, target, loads.at[n])
        for n, (source, target) in enumerate(zip(sources, targets))
    ]
    for copy in copies[:5]:
        copy.start()

    i = lax.axis_index("px")
    j = lax.axis_index("py")
    me = i * N_PY + j
    neighbours = [
        (i > 0, (jnp.maximum(i - 1, 0), j)),
        (i < N_PX - 1, (jnp.minimum(i + 1, N_PX - 1), j)),
        (j > 0, (i, jnp.maximum(j - 1, 0))),
        (j < N_PY - 1, (i, jnp.minimum(j + 1, N_PY - 1))),
    ]
    facing = [1, 0, 3, 2]

    halo_in[...] = jnp.zeros_like(halo_in)
    back_in[...] = jnp.zeros_like(back_in)

    barrier = pltpu.get_barrier_semaphore()

    flips = [
        j + sum((1 - 2 * lax.rem(j // (1 << b), 2)) * (1 << b) for b in range(3) if mask >> b & 1)
        for mask in range(N_PY)
    ]

    def flip(mask):
        return sum(lax.rem(i // (1 << b) + mask // (1 << b), 2) * (1 << b) for b in range(4))

    def everyone(act):
        for mask in range(N_PX - 1, 0, -1):
            px = flip(mask)
            for py in flips[::-1]:
                act(px, py)
        for py in flips[:0:-1]:
            act(i, py)

    def greet(px, py):
        pl.semaphore_signal(barrier, inc=1, device_id=(px, py), device_id_type=MESH)

    everyone(greet)
    for copy in copies[5:]:
        copy.start()

    def to_rows(source, target, count, rows):
        for c in range(count):
            for r in range(rows):
                target[pl.ds(c * rows + r, 1), :] = source[
                    pl.ds(c, 1), pl.ds(r * LANES, LANES)
                ]

    devs = iota((LANES, LANES), 0)
    lanes = iota((LANES, LANES), 1)
    earlier = jnp.concatenate(
        [jnp.where(devs < lanes, 1.0, 0.0), jnp.ones((LANES, LANES), F32)], axis=1
    ).astype(BF16)
    copies[0].wait()
    before = jnp.zeros((LANES, LANES), F32)
    named, ranks = [], []
    for row in range(CROW):
        here = jnp.broadcast_to(bucket[pl.ds(row, 1), :], (LANES, LANES)) == devs
        ones = jnp.where(here, 1.0, 0.0).astype(BF16)
        counts = jnp.dot(ones, earlier, preferred_element_type=F32)
        ranks.append(
            jnp.sum(jnp.where(here, counts[:, :LANES] + before, 0.0), axis=0, keepdims=True)
        )
        before = before + counts[:, LANES:]
        named.append(ones)

    copies[1].wait()
    slot_row = (devs & (CAP - 1)).astype(F32)
    nodes = jnp.zeros((LANES, 2 * LANES), F32)
    for row in range(0, CROW, 2):
        right = []
        for one in (row, row + 1):
            here = jnp.broadcast_to(ranks[one], (LANES, LANES)) == slot_row
            node = contact_nodes[pl.ds(one, 1), :]
            low = jnp.broadcast_to((node & (LANES - 1)).astype(F32), (LANES, LANES))
            high = jnp.broadcast_to(((node >> 7) + 1).astype(F32), (LANES, LANES))
            right.append(
                jnp.concatenate(
                    [jnp.where(here, low, 0.0), jnp.where(here, high, 0.0)], axis=0
                ).astype(BF16)
            )
        nodes = nodes + lax.dot_general(
            jnp.concatenate([named[row], named[row + 1]], axis=1),
            jnp.concatenate(right, axis=1),
            (((1,), (1,)), ((), ())),
            preferred_element_type=F32,
        )
    inverse[pl.ds(0, DEVS), :] = nodes[:, :LANES]
    inverse[pl.ds(DEVS, DEVS), :] = nodes[:, LANES:]
    block = iota((SROW, LANES), 1) >> 5
    low = jnp.zeros((SROW, LANES), F32)
    high = jnp.zeros((SROW, LANES), F32)
    for q in range(4):
        low = jnp.where(block == q, inverse[pl.ds(q, SROW, stride=4), :], low)
        high = jnp.where(block == q, inverse[pl.ds(DEVS + q, SROW, stride=4), :], high)
    slot_low[...] = low.astype(I32)
    slot_high[...] = high.astype(I32) - 1
    build_onehots(slot_low, 0, SROW, onehot, IDXROW // 2)

    copies[2].wait()
    copies[3].wait()
    to_rows(coords, base, 3, NROW)
    to_rows(displacement, disp, 3, NROW)

    def prepare_halo():
        copies[4].wait()
        for k in range(4):
            for r in range(HROW):
                entry = halo_lists[pl.ds(k, 1), pl.ds(r * LANES, LANES)]
                idx_low[pl.ds(4 * EROW + k * HROW + r, 1), :] = entry & (LANES - 1)
                idx_high[pl.ds(4 * EROW + k * HROW + r, 1), :] = entry >> 7
        build_onehots(idx_low, 4 * EROW, 4 * HROW, onehot, 2 * EROW)

    def prepare_rest():
        for copy in copies[5:]:
            copy.wait()
        for k in range(4):
            for r in range(EROW):
                entry = elem_nodes[pl.ds(k, 1), pl.ds(r * LANES, LANES)]
                idx_low[pl.ds(k * EROW + r, 1), :] = entry & (LANES - 1)
                idx_high[pl.ds(k * EROW + r, 1), :] = entry >> 7
        build_onehots(idx_low, 0, 4 * EROW, onehot, 0)
        to_rows(velocity, vel, 3, NROW)
        to_rows(ext_force, fext, 3, NROW)
        for r in range(EROW):
            slow[pl.ds(r, 1), :] = jnp.full((1, LANES), block_class[r], I32)
        for column in range(12):
            spread[pl.ds(column * 16, 12), :] = jnp.broadcast_to(
                stiffness[:, column : column + 1], (12, LANES)
            )

    def exchange_start(number, source, target, sent, got):
        for n, (exists, device) in enumerate(neighbours):

            @pl.when(exists)
            def _():
                pltpu.make_async_remote_copy(
                    src_ref=source.at[number, n],
                    dst_ref=target.at[number, facing[n]],
                    send_sem=sent.at[number, n],
                    recv_sem=got.at[number, facing[n]],
                    device_id=device,
                    device_id_type=MESH,
                ).start()

    def exchange_wait(number, buffer, sem):
        for n, (exists, _unused) in enumerate(neighbours):

            @pl.when(exists)
            def _():
                pltpu.make_async_copy(
                    buffer.at[number, n], buffer.at[number, n], sem.at[number, n]
                ).wait()

    def slots_start(number):
        def send(px, py):
            pltpu.make_async_remote_copy(
                src_ref=slots_out.at[number, px * N_PY + py],
                dst_ref=slots_in.at[number, me],
                send_sem=slots_sent.at[number],
                recv_sem=slots_got.at[number],
                device_id=(px, py),
                device_id_type=MESH,
            ).start()

        everyone(send)
        slots_in[number, me] = slots_out[number, me]

    def slots_wait(number, buffer, sem):
        part = buffer.at[number, pl.ds(0, DEVS - 1)]
        pltpu.make_async_copy(part, part, sem.at[number]).wait()

    def to_messages(parts, number):
        for q in range(4):
            mixed = jnp.zeros((SROW, LANES), F32)
            for c in range(3):
                shift = (CAP * (c - q)) % LANES
                turned = pltpu.roll(parts[c], shift, 1) if shift else parts[c]
                mixed = jnp.where(block == c, turned, mixed)
            stage[pl.ds(q * SROW, SROW), :] = mixed
        for a in range(SROW):
            for q in range(4):
                slots_out[number, 4 * a + q] = stage[pl.ds(q * SROW + a, 1), :]

    def from_messages(number):
        for a in range(SROW):
            for q in range(4):
                stage[pl.ds(q * SROW + a, 1), :] = slots_in[number, 4 * a + q]
        parts = []
        for c in range(3):
            mixed = jnp.zeros((SROW, LANES), F32)
            for q in range(4):
                shift = (CAP * (q - c)) % LANES
                rows = stage[pl.ds(q * SROW, SROW), :]
                turned = pltpu.roll(rows, shift, 1) if shift else rows
                mixed = jnp.where(block == q, turned, mixed)
            parts.append(mixed)
        return parts

    def send_points(number):
        gather(
            split_table(base[...] + disp[...]),
            0,
            SROW,
            slot_high,
            0,
            onehot,
            IDXROW // 2,
            points,
            0,
            False,
        )
        empty = slot_high[...] < 0
        to_messages(
            [jnp.where(empty, FAR, points[pl.ds(c * SROW, SROW), :]) for c in range(3)],
            number,
        )

    def push_tiles(number):
        for c, part in enumerate(from_messages(number)):
            points[pl.ds(c * SROW, SROW), :] = part
        numbers = iota((SROW, LANES), 0)

        def some_pairs(step, totals):
            for inner in range(PAIR_UNROLL):
                totals = one_pair(step * PAIR_UNROLL + inner, totals)
            return totals

        def one_pair(p, totals):
            first = tile_pairs[0, p]
            second = tile_pairs[1, p]
            mine = [
                jnp.broadcast_to(points[pl.ds(c * SROW + first, 1), :], (8, LANES))
                for c in range(3)
            ]
            others = [
                jnp.broadcast_to(points[pl.ds(c * SROW + second, 1), :], (8, LANES))
                for c in range(3)
            ]
            sums = [jnp.zeros((8, LANES), F32) for c in range(3)]
            for turn in range(LANES // 8):
                gap = [
                    mine[c] - pltpu.roll(others[c], turn * 8, 1, stride=1, stride_axis=0)
                    for c in range(3)
                ]
                dist = gap[0] * gap[0] + gap[1] * gap[1] + gap[2] * gap[2]
                weight = PENALTY * jnp.exp(dist * (-1.0 / REACH))
                sums = [sums[c] + weight * gap[c] for c in range(3)]
            return tuple(
                totals[c]
                + jnp.where(numbers == first, jnp.sum(sums[c], axis=0, keepdims=True), 0.0)
                for c in range(3)
            )

        zero = jnp.zeros((SROW, LANES), F32)
        return lax.fori_loop(0, PAIRS // PAIR_UNROLL, some_pairs, (zero, zero, zero))

    def list_edges(number):
        gather(
            split_table(disp[...]),
            0,
            4 * HROW,
            idx_high,
            4 * EROW,
            onehot,
            2 * EROW,
            returned,
            0,
            False,
        )
        for n in range(4):
            for c in range(3):
                halo_out[number, n, pl.ds(c * HROW, HROW), :] = returned[
                    pl.ds((c * 4 + n) * HROW, HROW), :
                ]

    def send_edges(number):
        exchange_start(number, halo_out, halo_in, halo_sent, halo_got)

    def own_corners():
        gather(
            split_table(disp[...]), 0, 4 * EROW, idx_high, 0, onehot, 0, found, 0, False
        )

    def element_stage(number, sub_no):
        exchange_wait(number, halo_in, halo_got)
        for n in range(4):
            for c in range(3):
                ghosts[pl.ds((c * 4 + n) * HROW, HROW), :] = halo_in[
                    number, n, pl.ds(c * HROW, HROW), :
                ]
        gather(
            split_table(ghosts[...]), NROW, 4 * EROW, idx_high, 0, onehot, 0, found, 0, True
        )
        local = [found[pl.ds(n * EROW, EROW), :] for n in range(12)]
        thick = thickness[...]
        for out in range(12):
            total = jnp.zeros((EROW, LANES), F32)
            for of in range(12):
                factor = spread[pl.ds(of * 16 + out, 1), :]
                total = total + jnp.broadcast_to(factor, (EROW, LANES)) * local[of]
            total = thick * total
            place = pl.ds(out * EROW, EROW)
            if sub_no == 0:
                held[place, :] = total
            else:
                total = jnp.where(slow[...] == 1, held[place, :], total)
            forces[place, :] = total
        halve(forces, halved, 4 * EROW)
        summed = scatter(halved, 4 * EROW, idx_high, 0, onehot, 0, NROW)
        for c in range(3):
            for n in range(4):
                first = (c * 4 + n) * HROW
                back_out[number, n, pl.ds(c * HROW, HROW), :] = summed[first : first + HROW]
        exchange_start(number, back_out, back_in, back_sent, back_got)

    def own_sums():
        internal[...] = scatter(halved, 4 * EROW, idx_high, 0, onehot, 0, 0)

    def return_stage(number):
        exchange_wait(number, back_in, back_got)
        for n in range(4):
            for c in range(3):
                returned[pl.ds(c * 4 * HROW + n * HROW, HROW), :] = back_in[
                    number, n, pl.ds(c * HROW, HROW), :
                ]
        halve(returned, halved, 4 * HROW)
        internal[...] = internal[...] + scatter(
            halved, 4 * HROW, idx_high, 4 * EROW, onehot, 2 * EROW, 0
        )

    def update():
        mass = inv_mass[...]
        for c in range(3):
            place = pl.ds(c * NROW, NROW)
            accel = mass * (fext[place, :] - internal[place, :] + contact[place, :])
            last[pl.ds(c * NROW, NROW), :] = disp[place, :]
            last[pl.ds((3 + c) * NROW, NROW), :] = vel[place, :]
            last[pl.ds((6 + c) * NROW, NROW), :] = accel
            speed = vel[place, :] + DT * accel
            vel[place, :] = speed
            disp[place, :] = disp[place, :] + DT * speed

    def major(step, carry):
        there, back = 2 * step, 2 * step + 1
        pl.when(step == 0)(prepare_halo)
        list_edges(there)
        send_points(there)

        @pl.when(step == 0)
        def _():
            pl.semaphore_wait(barrier, DEVS - 1)

        send_edges(there)
        slots_start(there)
        pl.when(step == 0)(prepare_rest)
        own_corners()
        element_stage(there, 0)
        slots_wait(there, slots_in, slots_got)
        to_messages(push_tiles(there), back)
        slots_start(back)
        own_sums()
        return_stage(there)
        slots_wait(back, slots_in, slots_got)
        for c, part in enumerate(from_messages(back)):
            pushes[pl.ds(c * SROW, SROW), :] = part
        halve(pushes, halved, SROW)
        contact[...] = scatter(halved, SROW, slot_high, 0, onehot, IDXROW // 2, 0)
        update()
        for sub_no in range(1, SUBS):
            list_edges(back)
            send_edges(back)
            own_corners()
            element_stage(back, sub_no)
            own_sums()
            return_stage(back)
            update()
        return carry

    lax.fori_loop(0, STEPS, major, 0)

    for c in range(3):
        for r in range(NROW):
            place = pl.ds(r * LANES, LANES)
            for n, out in enumerate((disp_out, vel_out, accel_out)):
                out[pl.ds(c, 1), place] = last[pl.ds((n * 3 + c) * NROW + r, 1), :]

    def drain(number, carry):
        exchange_wait(number, halo_out, halo_sent)
        exchange_wait(number, back_out, back_sent)
        slots_wait(number, slots_out, slots_sent)
        return carry

    lax.fori_loop(0, STEPS * SUBS, drain, 0)


def device_step(
    coords,
    displacement,
    velocity,
    inv_mass,
    ext_force,
    thickness,
    stiffness,
    elem_nodes,
    block_class,
    halo_lists,
    contact_nodes,
    contact_bucket,
    tile_pairs,
):
    times = STEPS * SUBS
    vmem = pl.BlockSpec(memory_space=pltpu.VMEM)
    apart = pl.BlockSpec(memory_space=pltpu.HBM)
    dma = pltpu.SemaphoreType.DMA
    shape = jax.ShapeDtypeStruct(coords.shape, F32)
    rows = lambda count, kind=F32: pltpu.VMEM((count, LANES), kind)
    field = pltpu.VMEM(coords.shape, F32)
    edges = pltpu.VMEM((times, 4, 3 * HROW, LANES), F32)
    messages = pltpu.VMEM((times, DEVS, 1, LANES), F32)
    disp, vel, accel = pl.pallas_call(
        body,
        out_shape=(shape, shape, shape),
        in_specs=[apart] * 13,
        out_specs=(vmem, vmem, vmem),
        scratch_shapes=[
            field,
            field,
            field,
            field,
            pltpu.VMEM(elem_nodes.shape, I32),
            pltpu.VMEM(halo_lists.shape, I32),
            rows(NROW),
            rows(EROW),
            rows(CROW, I32),
            rows(CROW, I32),
            pltpu.VMEM(stiffness.shape, F32),
            pltpu.SMEM(block_class.shape, I32),
            pltpu.SMEM(tile_pairs.shape, I32),
            rows(3 * NROW),
            rows(3 * NROW),
            rows(3 * NROW),
            rows(3 * NROW),
            rows(9 * NROW),
            rows(EROW, I32),
            rows(12 * 16),
            rows(IDXROW, I32),
            rows(IDXROW, I32),
            rows(12 * EROW),
            rows(12 * EROW),
            rows(12 * EROW),
            rows(24 * EROW),
            rows(3 * NROW),
            rows(3 * NROW),
            rows(12 * HROW),
            rows(12 * HROW),
            pltpu.VMEM(((IDXROW + SROW) // 2, LANES, 2 * LANES), BF16),
            rows(2 * DEVS),
            rows(SROW, I32),
            rows(SROW, I32),
            rows(3 * SROW),
            rows(3 * SROW),
            rows(DEVS),
            edges,
            edges,
            edges,
            edges,
            messages,
            messages,
            dma((13,)),
            dma((times, 4)),
            dma((times, 4)),
            dma((times, 4)),
            dma((times, 4)),
            dma((times,)),
            dma((times,)),
        ],
        compiler_params=pltpu.CompilerParams(
            collective_id=0, has_side_effects=True, vmem_limit_bytes=60 * 1024 * 1024
        ),
    )(
        coords,
        displacement,
        velocity,
        ext_force,
        elem_nodes,
        halo_lists,
        inv_mass.reshape(NROW, LANES),
        thickness.reshape(EROW, LANES),
        contact_nodes.reshape(CROW, LANES),
        contact_bucket.reshape(CROW, LANES),
        stiffness,
        block_class,
        tile_pairs,
    )
    vel = vel + DT * accel
    return disp + DT * vel, vel


def solution(mesh):
    split = P(None, ("px", "py"))
    line = P(("px", "py"))
    placed = (
        split,
        split,
        split,
        line,
        split,
        line,
        P(),
        split,
        line,
        split,
        line,
        P(("px", "py"), None),
        split,
    )
    return jax.shard_map(
        device_step,
        mesh=mesh,
        in_specs=placed,
        out_specs=(split, split),
        check_vma=False,
    )
```
